32 devices in a mesh: dp: 8 (over z, core), seq: 4 (over y, x).
Axes of the slice: x: 2, y: 2, z: 4, core: 2. Of those that a mesh axis runs over, the one named last changes fastest.
Arguments:
- hidden: bfloat16 [8, 2, 256, 8192], P('dp', None, 'seq'), may hold values from -6 to 6
- queries: bfloat16 [8, 2, 256, 4096], P('dp', None, 'seq'), may hold values from -240 to 240
- key_matrix: bfloat16 [8192, 1024], P('dp', 'seq'), may hold values from -0.0625 to 0.0625
- value_matrix: bfloat16 [8192, 1024], P('dp', 'seq'), may hold values from -0.0625 to 0.0625
- out_grad: bfloat16 [8, 2, 256, 4096], P('dp', None, 'seq'), may hold values from -6 to 6
Outputs:
- attn_out: bfloat16 [8, 2, 256, 4096], P('dp', None, 'seq')
- query_grad: bfloat16 [8, 2, 256, 4096], P('dp', None, 'seq')
- key_weight_grad: float32 [8192, 1024], P('dp', 'seq')
- value_weight_grad: float32 [8192, 1024], P('dp', 'seq')
The draws below stay inside these ranges and needn't reach their ends.
All inputs are finite; a program needn't handle non-finite values.
Results may differ from the reference program's by a relative error of at most 0.025.
The reference program's roundings to bfloat16 on the way count: a program that leaves them out, or rounds other values in their place, can miss the bound.
Values may be sent and summed in bfloat16 or wider, within the bound.
A program may use at most 128 MiB of HBM per device.

```python
import math
import jax
import jax.numpy as jnp
from jax import lax

EMBED_WIDTH = 8192
QUERY_HEADS_HALF = 32
KEY_VALUE_HEADS = 8
HEAD_WIDTH = 128
STRETCHES = 2
STRETCH = 256
BATCH = 8


def draw_queries(key, part):
    base_key = jax.random.fold_in(jax.random.fold_in(key, 7), 0)
    base = jax.random.truncated_normal(base_key, -6.0, 6.0, (BATCH, STRETCHES, STRETCH, QUERY_HEADS_HALF * HEAD_WIDTH), jnp.float32)
    return base.astype(jnp.bfloat16)


def block_levels(key, shape, cuts, low, top_value):
    loudness, own = 1.0, jax.random.fold_in(key, 6)
    for position, shards_of in cuts:
        steps = jnp.exp(jax.random.uniform(jax.random.fold_in(own, position), (shards_of,), jnp.float32, low / len(cuts), top_value / len(cuts)))
        loudness = loudness * jnp.repeat(steps, shape[position] // shards_of).reshape([-1 if axis == position else 1 for axis in range(len(shape))])
    return loudness


def scatter_about(own_key, shape, width, reach, pieces=(), held_as=jnp.bfloat16):
    entries = jax.random.normal(own_key, shape, jnp.float32) * width
    if len(pieces) > 0:
        entries = block_levels(own_key, shape, pieces, -0.22, 0.18) * entries
    return jnp.clip(entries, min=-reach, max=reach).astype(held_as)


def setup_inputs(seed: int = 0) -> dict:
    key_of = jax.random.split(jax.random.key(seed), 6)
    return {
        "hidden": scatter_about(key_of[0], (BATCH, STRETCHES, STRETCH, EMBED_WIDTH), 1.0, 6.0, ((0, 8), (2, 4))),
        "queries": draw_queries(jax.random.fold_in(key_of[5], 71), 0),
        "key_matrix": scatter_about(key_of[2], (EMBED_WIDTH, KEY_VALUE_HEADS * HEAD_WIDTH), EMBED_WIDTH ** -0.5, 0.0625, ((0, 8), (1, 4))),
        "value_matrix": scatter_about(key_of[3], (EMBED_WIDTH, KEY_VALUE_HEADS * HEAD_WIDTH), EMBED_WIDTH ** -0.5, 0.0625, ((0, 8), (1, 4))),
        "out_grad": scatter_about(key_of[4], (BATCH, STRETCHES, STRETCH, QUERY_HEADS_HALF * HEAD_WIDTH), 1.0, 6.0, ((0, 8), (2, 4))),
    }


ROPE_BASE = 500000.0

def angle_tables(count, model_head):
    places = jnp.arange(count, dtype=jnp.float32)
    inverse = jnp.exp(jnp.arange(model_head // 2, dtype=jnp.float32) * (-2.0 * math.log(ROPE_BASE) / model_head))
    phase_table = places[:, None] * inverse[None, :]
    return (jnp.cos(phase_table), jnp.sin(phase_table))

def rotate(vector, cosine_lookup, sine_lookup):
    half_width = vector.shape[-1] // 2
    first_half = vector[..., :half_width]
    second_half = vector[..., half_width:]
    return jnp.concatenate([first_half * cosine_lookup - second_half * sine_lookup, second_half * cosine_lookup + first_half * sine_lookup], axis=-1)

def unrotate_gradient(vector, cosine_lookup, sine_lookup):
    half_width = vector.shape[-1] // 2
    first_half = vector[..., :half_width]
    second_half = vector[..., half_width:]
    return jnp.concatenate([first_half * cosine_lookup + second_half * sine_lookup, second_half * cosine_lookup - first_half * sine_lookup], axis=-1)

def reference(hidden, queries, key_matrix, value_matrix, out_grad):
    heads_per_group = QUERY_HEADS_HALF // KEY_VALUE_HEADS
    combined_length = STRETCHES * STRETCH
    score_scale = 1.0 / math.sqrt(HEAD_WIDTH)
    cosine_lookup, sine_lookup = angle_tables(combined_length, HEAD_WIDTH)
    cosine_lookup = cosine_lookup[:, None, :]
    sine_lookup = sine_lookup[:, None, :]
    allowed = jnp.arange(combined_length)[None, :] <= jnp.arange(combined_length)[:, None]

    def one_sequence(running, inputs):
        token_inputs, query_sequence, gradient_sequence = inputs
        token_inputs = token_inputs.reshape(combined_length, EMBED_WIDTH)
        query_whole = query_sequence.reshape(combined_length, KEY_VALUE_HEADS, heads_per_group, HEAD_WIDTH).astype(jnp.float32)
        gradient_whole = gradient_sequence.reshape(combined_length, KEY_VALUE_HEADS, heads_per_group, HEAD_WIDTH).astype(jnp.float32)
        key_projected_raw = jnp.dot(token_inputs, key_matrix, preferred_element_type=jnp.float32).reshape(combined_length, KEY_VALUE_HEADS, HEAD_WIDTH)
        key_half = rotate(key_projected_raw, cosine_lookup, sine_lookup).astype(jnp.bfloat16)
        key_cache = lax.optimization_barrier(key_half).astype(jnp.float32)
        value_stretch_half = jnp.dot(token_inputs, value_matrix, preferred_element_type=jnp.float32).astype(jnp.bfloat16)
        cached_values = lax.optimization_barrier(value_stretch_half).astype(jnp.float32).reshape(combined_length, KEY_VALUE_HEADS, HEAD_WIDTH)
        scores = jnp.einsum('tkgd,skd->kgts', query_whole, key_cache) * score_scale
        scores = jnp.where(allowed[None, None], scores, -jnp.inf)
        row_peak = lax.optimization_barrier(jnp.max(scores, axis=-1, keepdims=True))
        exp_scores = jnp.exp(scores - row_peak)
        prob_full = exp_scores / lax.optimization_barrier(jnp.sum(exp_scores, axis=-1, keepdims=True))
        prob_half = lax.optimization_barrier(prob_full.astype(jnp.bfloat16)).astype(jnp.float32)
        attended = jnp.einsum('kgts,skd->tkgd', prob_half, cached_values).astype(jnp.bfloat16)
        attended_wide = lax.optimization_barrier(attended).astype(jnp.float32)
        grad_prob = jnp.einsum('tkgd,skd->kgts', gradient_whole, cached_values)
        row_dot = jnp.einsum('tkgd,tkgd->kgt', gradient_whole, attended_wide)
        grad_score = (prob_full * (grad_prob - row_dot[..., None]) * score_scale).astype(jnp.bfloat16)
        grad_score = lax.optimization_barrier(grad_score).astype(jnp.float32)
        query_grad_seq = jnp.einsum('kgts,skd->tkgd', grad_score, key_cache).astype(jnp.bfloat16)
        key_gradient = jnp.einsum('kgts,tkgd->skd', grad_score, query_whole)
        value_gradient = jnp.einsum('kgts,tkgd->skd', prob_half, gradient_whole)
        key_unrotated = unrotate_gradient(key_gradient, cosine_lookup, sine_lookup).astype(jnp.bfloat16).reshape(combined_length, KEY_VALUE_HEADS * HEAD_WIDTH)
        value_projected = value_gradient.astype(jnp.bfloat16).reshape(combined_length, KEY_VALUE_HEADS * HEAD_WIDTH)
        key_term = jnp.dot(token_inputs.T, key_unrotated, preferred_element_type=jnp.float32)
        value_term = jnp.dot(token_inputs.T, value_projected, preferred_element_type=jnp.float32)
        outputs = (attended.reshape(STRETCHES, STRETCH, QUERY_HEADS_HALF * HEAD_WIDTH), query_grad_seq.reshape(STRETCHES, STRETCH, QUERY_HEADS_HALF * HEAD_WIDTH))
        return ((running[0] + key_term, running[1] + value_term), outputs)
    leading_gradients = (jnp.zeros((EMBED_WIDTH, KEY_VALUE_HEADS * HEAD_WIDTH), jnp.float32), jnp.zeros((EMBED_WIDTH, KEY_VALUE_HEADS * HEAD_WIDTH), jnp.float32))
    (key_weight_grad, value_weight_grad), (attn_out, query_grad) = lax.scan(one_sequence, leading_gradients, (hidden, queries, out_grad))
    return (attn_out, query_grad, key_weight_grad, value_weight_grad)
```

```python
import functools
import math

import jax
import jax.numpy as jnp
import numpy as np
from jax import lax
from jax.experimental import pallas as pl
from jax.experimental.pallas import tpu as pltpu
from jax.sharding import PartitionSpec as P

HEAD_WIDTH = 128
ROPE_BASE = 500000.0
CORES = 2
MESH = pl.DeviceIdType.MESH
ANY = pl.BlockSpec(memory_space=pl.ANY)
VMEM = pl.BlockSpec(memory_space=pltpu.VMEM)
VMEM_LIMIT = 60 << 20


def grid_of(count):
    rows = 2 if count % 2 == 0 else 1
    return rows, count // rows


def place(n_seq, n_dp):
    dp, seq = lax.axis_index("dp"), lax.axis_index("seq")
    chips = n_dp // CORES
    chip, core = lax.div(dp, CORES), lax.rem(dp, CORES)
    rows, cols = grid_of(n_seq)
    row, col = lax.div(seq, cols), lax.rem(seq, cols)
    row_peers = [row * cols + lax.rem(col + d, cols) for d in range(1, cols)]
    col_peers = [lax.rem(row + d, rows) * cols + col for d in range(1, rows)]
    far_peers = [
        lax.rem(row + e, rows) * cols + lax.rem(col + d, cols)
        for e in range(1, rows)
        for d in range(1, cols)
    ]
    return dp, seq, chips, chip, core, row_peers, col_peers, far_peers


def greet(dp, seq, chips, chip, core, peers):
    barrier = pltpu.get_barrier_semaphore()
    ids = [(dp, p) for p in peers]
    ids.append((chip * CORES + 1 - core, seq))
    if chips > 1:
        for d in (1, chips - 1):
            ids.append((lax.rem(chip + d, chips) * CORES + core, seq))
    for device in ids:
        pl.semaphore_signal(barrier, inc=1, device_id=device, device_id_type=MESH)
    pl.semaphore_wait(barrier, len(ids))


def gather_kernel(
    n_seq, n_dp, hidden, queries, key_matrix, value_matrix, out_grad,
    hid_all, qry_all, grd_all, key_all, val_all,
    hid_own, qry_own, grd_own, key_own, val_own,
    load_sem, store_sem, hid_send, hid_recv, qry_send, qry_recv, grd_send, grd_recv,
    up_send, down_send, mate_send, w_recv,
):
    dp, seq, chips, chip, core, row_peers, col_peers, far_peers = place(n_seq, n_dp)
    peers = row_peers + col_peers + far_peers
    width = qry_own.shape[2]
    mine = pl.ds(pl.multiple_of(seq * width, width), width)
    local_pairs = (
        (hidden, hid_own, hid_all.at[:, seq]),
        (queries.at[:, :, mine], qry_own, qry_all.at[:, seq]),
        (out_grad.at[:, :, mine], grd_own, grd_all.at[:, seq]),
        (key_matrix, key_own, key_all.at[dp]),
        (value_matrix, val_own, val_all.at[dp]),
    )
    for i, (src, tmp, _) in enumerate(local_pairs):
        pltpu.make_async_copy(src, tmp, load_sem.at[i]).start()
    greet(dp, seq, chips, chip, core, peers)
    sends = []
    slots = iter(range(hid_send.shape[0]))

    def send_hidden(source, half, target, src):
        copy = pltpu.make_async_remote_copy(
            src_ref=src, dst_ref=hid_all.at[half, source],
            send_sem=hid_send.at[next(slots)], recv_sem=hid_recv.at[source, half],
            device_id=(dp, target), device_id_type=MESH,
        )
        copy.start()
        sends.append(copy)

    def wait_hidden(source, half):
        pltpu.make_async_remote_copy(
            src_ref=hid_all.at[half, source], dst_ref=hid_all.at[half, source],
            send_sem=hid_send.at[0], recv_sem=hid_recv.at[source, half],
            device_id=(dp, source), device_id_type=MESH,
        ).wait_recv()

    tables = (key_all, val_all)
    owns = (key_matrix, value_matrix)

    def weight_copy(kind, piece, target_dp, send_sem, own=False):
        return pltpu.make_async_remote_copy(
            src_ref=owns[kind] if own else tables[kind].at[piece],
            dst_ref=tables[kind].at[piece],
            send_sem=send_sem, recv_sem=w_recv.at[piece, kind],
            device_id=(target_dp, seq), device_id_type=MESH,
        )

    above, below = dp + CORES, dp - CORES
    mate = chip * CORES + 1 - core
    has_above, has_below = chip < chips - 1, chip > 0

    def go(cond, copy_of, wait=False):
        @pl.when(cond)
        def _():
            copy = copy_of()
            copy.wait_send() if wait else copy.start()

    for p in row_peers:
        send_hidden(seq, 0, p, hidden.at[0])
    for p in col_peers:
        send_hidden(seq, 1, p, hidden.at[1])
    for kind in range(2):
        go(has_above, lambda: weight_copy(kind, dp, above, up_send.at[0, kind], True))
        go(has_below, lambda: weight_copy(kind, dp, below, down_send.at[0, kind], True))
    for p in row_peers:
        send_hidden(seq, 1, p, hidden.at[1])
    for p in col_peers:
        send_hidden(seq, 0, p, hidden.at[0])
    for kind in range(2):
        weight_copy(kind, dp, mate, mate_send.at[dp, kind], True).start()
    for i, (src, tmp, dst) in enumerate(local_pairs):
        pltpu.make_async_copy(src, tmp, load_sem.at[i]).wait()
        pltpu.make_async_copy(tmp, dst, store_sem.at[i]).start()

    def relay_weight(step, kind):
        low, high = dp - CORES * step, dp + CORES * step

        @pl.when(chip >= step)
        def _():
            weight_copy(kind, low, below, up_send.at[step, kind]).wait_recv()
            go(has_above, lambda: weight_copy(kind, low, above, up_send.at[step, kind]))
            weight_copy(kind, low, mate, mate_send.at[low, kind]).start()

        @pl.when(chip + step < chips)
        def _():
            weight_copy(kind, high, above, down_send.at[step, kind]).wait_recv()
            go(has_below, lambda: weight_copy(kind, high, below, down_send.at[step, kind]))
            weight_copy(kind, high, mate, mate_send.at[high, kind]).start()

    def relay_hidden():
        for p in row_peers:
            wait_hidden(p, 0)
            for q in col_peers:
                send_hidden(p, 0, q, hid_all.at[0, p])
        for p in col_peers:
            wait_hidden(p, 1)
            for q in row_peers:
                send_hidden(p, 1, q, hid_all.at[1, p])

    def exchange(src, dst, send_sem, recv_sem):
        for i, p in enumerate(peers):
            cols = pl.ds(pl.multiple_of(p * width, width), width)
            copy = pltpu.make_async_remote_copy(
                src_ref=src.at[:, :, cols], dst_ref=dst.at[:, seq],
                send_sem=send_sem.at[i], recv_sem=recv_sem.at[seq],
                device_id=(dp, p), device_id_type=MESH,
            )
            copy.start()
            sends.append(copy)

    def wait_exchange(dst, send_sem, recv_sem):
        for p in peers:
            pltpu.make_async_remote_copy(
                src_ref=dst.at[:, p], dst_ref=dst.at[:, p],
                send_sem=send_sem.at[0], recv_sem=recv_sem.at[p],
                device_id=(dp, p), device_id_type=MESH,
            ).wait_recv()

    if chips > 1:
        relay_weight(1, 0)
    relay_hidden()
    exchange(queries, qry_all, qry_send, qry_recv)
    exchange(out_grad, grd_all, grd_send, grd_recv)
    if chips > 1:
        relay_weight(1, 1)
    for step in range(2, chips):
        for kind in range(2):
            relay_weight(step, kind)
    for p in row_peers:
        wait_hidden(p, 1)
    for p in col_peers:
        wait_hidden(p, 0)
    for p in far_peers:
        wait_hidden(p, 0)
        wait_hidden(p, 1)
    wait_exchange(qry_all, qry_send, qry_recv)
    wait_exchange(grd_all, grd_send, grd_recv)
    for other in range(chips):
        for kind in range(2):
            piece = other * CORES + 1 - core
            weight_copy(kind, piece, mate, mate_send.at[piece, kind]).wait_recv()
    for copy in sends:
        copy.wait_send()
    for kind in range(2):
        for step in range(max(chips - 1, 1)):
            low, high = dp - CORES * step, dp + CORES * step
            go(jnp.logical_and(has_above, chip >= step),
               lambda: weight_copy(kind, low, above, up_send.at[step, kind]), True)
            go(jnp.logical_and(has_below, chip + step < chips),
               lambda: weight_copy(kind, high, below, down_send.at[step, kind]), True)
        for other in range(chips):
            piece = other * CORES + core
            weight_copy(kind, piece, mate, mate_send.at[piece, kind]).wait_send()
    for i, (_, tmp, dst) in enumerate(local_pairs):
        pltpu.make_async_copy(tmp, dst, store_sem.at[i]).wait()


def gather_all(n_seq, n_dp, hidden, queries, key_matrix, value_matrix, out_grad):
    _, stretches, tokens, embed = hidden.shape
    width = queries.shape[3] // n_seq
    chips = n_dp // CORES
    rows, cols = grid_of(n_seq)
    hid_sends = 2 * (rows - 1 + cols - 1) + 2 * (rows - 1) * (cols - 1)
    bf16 = jnp.bfloat16
    dma = pltpu.SemaphoreType.DMA
    heads = (stretches, n_seq, tokens, width)
    own = (stretches, tokens, width)
    weight = key_matrix.shape
    return pl.pallas_call(
        functools.partial(gather_kernel, n_seq, n_dp),
        out_shape=[
            jax.ShapeDtypeStruct((stretches, n_seq, tokens, embed), bf16),
            jax.ShapeDtypeStruct(heads, bf16),
            jax.ShapeDtypeStruct(heads, bf16),
            jax.ShapeDtypeStruct((n_dp,) + weight, bf16),
            jax.ShapeDtypeStruct((n_dp,) + weight, bf16),
        ],
        in_specs=[ANY] * 5,
        out_specs=[ANY] * 5,
        scratch_shapes=[
            pltpu.VMEM((stretches, tokens, embed), bf16),
            pltpu.VMEM(own, bf16),
            pltpu.VMEM(own, bf16),
            pltpu.VMEM(weight, bf16),
            pltpu.VMEM(weight, bf16),
            dma((5,)), dma((5,)),
            dma((hid_sends,)), dma((n_seq, 2)),
            dma((n_seq,)), dma((n_seq,)), dma((n_seq,)), dma((n_seq,)),
            dma((chips, 2)), dma((chips, 2)), dma((n_dp, 2)), dma((n_dp, 2)),
        ],
        compiler_params=pltpu.CompilerParams(
            collective_id=0, has_side_effects=True, vmem_limit_bytes=VMEM_LIMIT
        ),
        name="gather_all",
    )(hidden[0], queries[0], key_matrix, value_matrix, out_grad[0])


def attention_kernel(
    group, key_raw, val_raw, cos, sin, cos_t, sin_t, qry, grd,
    out, qry_grad, pre_t, keys, vals, key_acc, val_acc,
):
    member = pl.program_id(1)
    total = qry.shape[0]
    half = HEAD_WIDTH // 2
    block = total // 2
    scale = 1.0 / math.sqrt(HEAD_WIDTH)
    f32, bf16 = jnp.float32, jnp.bfloat16

    @pl.when(member == 0)
    def _():
        raw = key_raw[...]
        swapped = jnp.concatenate([raw[:, half:], raw[:, :half]], axis=1)
        keys[...] = (raw * cos[...] + swapped * sin[...]).astype(bf16)
        vals[...] = val_raw[...].astype(bf16)
        key_acc[...] = jnp.zeros_like(key_acc)
        val_acc[...] = jnp.zeros_like(val_acc)

    nt = (((1,), (1,)), ((), ()))
    tn = (((0,), (0,)), ((), ()))
    for b in range(2):
        rows = pl.ds(b * block, block)
        span = (b + 1) * block
        q, g = qry[rows, :], grd[rows, :]
        k, v = keys[:span, :], vals[:span, :]
        s = lax.dot_general(q, k, nt, preferred_element_type=f32) * scale
        at = b * block + lax.broadcasted_iota(jnp.int32, s.shape, 0)
        col = lax.broadcasted_iota(jnp.int32, s.shape, 1)
        s = jnp.where(col <= at, s, -jnp.inf)
        e = jnp.exp(s - jnp.max(s, axis=1, keepdims=True))
        p = e * (1.0 / jnp.sum(e, axis=1, keepdims=True))
        p_half = p.astype(bf16)
        o = jnp.dot(p_half, v, preferred_element_type=f32).astype(bf16)
        out[rows, :] = o
        dot = jnp.sum(g.astype(f32) * o.astype(f32), axis=1, keepdims=True)
        gp = lax.dot_general(g, v, nt, preferred_element_type=f32)
        ds = (p * (gp - dot) * scale).astype(bf16)
        qry_grad[rows, :] = jnp.dot(ds, k, preferred_element_type=f32).astype(bf16)
        key_acc[:, :span] += lax.dot_general(q, ds, tn, preferred_element_type=f32)
        val_acc[:, :span] += lax.dot_general(g, p_half, tn, preferred_element_type=f32)

    @pl.when(member == group - 1)
    def _():
        acc = key_acc[...]
        swapped = jnp.concatenate([acc[half:, :], acc[:half, :]], axis=0)
        pre_t[0] = (acc * cos_t[...] - swapped * sin_t[...]).astype(bf16)
        pre_t[1] = val_acc[...].astype(bf16)


def attention(key_raw, val_raw, qry, grd):
    total, width = qry.shape
    kv_width = key_raw.shape[1]
    kv_heads = kv_width // HEAD_WIDTH
    group = width // kv_width
    bf16, f32 = jnp.bfloat16, jnp.float32
    half = HEAD_WIDTH // 2
    inverse = np.exp(
        np.arange(half, dtype=np.float32) * np.float32(-2.0 * math.log(ROPE_BASE) / HEAD_WIDTH)
    ).astype(np.float32)
    phase = np.arange(total, dtype=np.float32)[:, None] * inverse[None, :]
    cos_half, sin_half = np.cos(phase), np.sin(phase)
    cos = np.concatenate([cos_half, cos_half], axis=1).astype(np.float32)
    sin = np.concatenate([-sin_half, sin_half], axis=1).astype(np.float32)
    head = lambda k, m: (0, k * group + m)
    by_kv = lambda k, m: (0, k)
    whole = lambda k, m: (0, 0)
    out, qry_grad, pre_t = pl.pallas_call(
        functools.partial(attention_kernel, group),
        grid=(kv_heads, group),
        in_specs=[
            pl.BlockSpec((total, HEAD_WIDTH), by_kv),
            pl.BlockSpec((total, HEAD_WIDTH), by_kv),
            pl.BlockSpec((total, HEAD_WIDTH), whole),
            pl.BlockSpec((total, HEAD_WIDTH), whole),
            pl.BlockSpec((HEAD_WIDTH, total), whole),
            pl.BlockSpec((HEAD_WIDTH, total), whole),
            pl.BlockSpec((total, HEAD_WIDTH), head),
            pl.BlockSpec((total, HEAD_WIDTH), head),
        ],
        out_specs=[
            pl.BlockSpec((total, HEAD_WIDTH), head),
            pl.BlockSpec((total, HEAD_WIDTH), head),
            pl.BlockSpec((2, HEAD_WIDTH, total), lambda k, m: (0, k, 0)),
        ],
        out_shape=[
            jax.ShapeDtypeStruct((total, width), bf16),
            jax.ShapeDtypeStruct((total, width), bf16),
            jax.ShapeDtypeStruct((2, kv_width, total), bf16),
        ],
        scratch_shapes=[
            pltpu.VMEM((total, HEAD_WIDTH), bf16),
            pltpu.VMEM((total, HEAD_WIDTH), bf16),
            pltpu.VMEM((HEAD_WIDTH, total), f32),
            pltpu.VMEM((HEAD_WIDTH, total), f32),
        ],
        compiler_params=pltpu.CompilerParams(
            dimension_semantics=("arbitrary", "arbitrary"), vmem_limit_bytes=VMEM_LIMIT
        ),
        name="attention",
    )(key_raw, val_raw, cos, sin, cos.T.copy(), sin.T.copy(), qry, grd)
    return out, qry_grad, pre_t.reshape(2 * kv_width, total)


def reduce_kernel(
    n_seq, n_dp, tile, hid, pre_t, attn, qgrad,
    attn_out, qgrad_out, weight_grad,
    attn_own, qgrad_own, acc, mate_out, mate_in, chain_out, down_in, up_in,
    load_sem, store_sem, a_send, a_recv, q_send, q_recv,
    mate_send, mate_recv, chain_send, down_recv, up_recv,
):
    dp, seq, chips, chip, core, row_peers, col_peers, far_peers = place(n_seq, n_dp)
    peers = row_peers + col_peers + far_peers
    width = attn_own.shape[2]
    height, depth = acc.shape[1], acc.shape[2]
    mine = pl.ds(pl.multiple_of(seq * width, width), width)
    local_pairs = (
        (attn.at[:, seq], attn_own, attn_out.at[:, :, mine]),
        (qgrad.at[:, seq], qgrad_own, qgrad_out.at[:, :, mine]),
    )
    for i, (src, tmp, _) in enumerate(local_pairs):
        pltpu.make_async_copy(src, tmp, load_sem.at[i]).start()
    greet(dp, seq, chips, chip, core, peers)
    exchanges = ((attn, attn_out, a_send, a_recv), (qgrad, qgrad_out, q_send, q_recv))
    sends = []
    for src, dst, send_sem, recv_sem in exchanges:
        for i, p in enumerate(peers):
            copy = pltpu.make_async_remote_copy(
                src_ref=src.at[:, p], dst_ref=dst.at[:, :, mine],
                send_sem=send_sem.at[i], recv_sem=recv_sem.at[seq],
                device_id=(dp, p), device_id_type=MESH,
            )
            copy.start()
            sends.append(copy)
    mate = chip * CORES + 1 - core

    def mate_copy(t):
        return pltpu.make_async_remote_copy(
            src_ref=mate_out.at[t], dst_ref=mate_in.at[t],
            send_sem=mate_send.at[t], recv_sem=mate_recv.at[t],
            device_id=(mate, seq), device_id_type=MESH,
        )

    def chain_copy(t, down):
        return pltpu.make_async_remote_copy(
            src_ref=chain_out.at[t], dst_ref=(down_in if down else up_in).at[t],
            send_sem=chain_send.at[t], recv_sem=(down_recv if down else up_recv).at[t],
            device_id=(dp - CORES if down else dp + CORES, seq), device_id_type=MESH,
        )

    def product(block, store):
        @pl.loop(0, depth // tile)
        def _(i):
            cols = pl.ds(pl.multiple_of(block * depth + i * tile, tile), tile)
            part = jnp.dot(pre_t[...], hid[:, cols], preferred_element_type=jnp.float32)
            store(pl.ds(pl.multiple_of(i * tile, tile), tile), part)

    @pl.loop(0, chips)
    def _(i):
        odd, k = lax.rem(i, 2), lax.div(i, 2)
        t = odd * (chips - 1 - k) + (1 - odd) * k

        def to_mate(cols, part):
            mate_out[t, :, cols] = part.astype(jnp.bfloat16)

        def to_acc(cols, part):
            acc[t, :, cols] = part

        product(t * CORES + 1 - core, to_mate)
        mate_copy(t).start()
        product(t * CORES + core, to_acc)

    strip = 64

    def sweep(fn):
        @pl.loop(0, height // strip)
        def _(i):
            fn(pl.ds(pl.multiple_of(i * strip, strip), strip))

    def take(t, extra):
        def fn(rows):
            acc[t, rows, :] += extra[t, rows, :].astype(jnp.float32)

        sweep(fn)

    def relay(t, down, has_input):
        mate_copy(t).wait_recv()
        take(t, mate_in)

        @pl.when(has_input)
        def _():
            chain_copy(t, down).wait_recv()
            take(t, down_in if down else up_in)

        def fn(rows):
            chain_out[t, rows, :] = acc[t, rows, :].astype(jnp.bfloat16)

        sweep(fn)
        chain_copy(t, down).start()

    has_above, has_below = chip < chips - 1, chip > 0

    @pl.loop(0, chips - 1)
    def _(tau):
        k_down = tau - (chips - 1 - chip)
        k_up = tau - chip

        @pl.when(jnp.logical_and(k_down >= 0, k_down < chip))
        def _():
            relay(k_down, True, has_above)

        @pl.when(jnp.logical_and(k_up >= 0, k_up < chips - 1 - chip))
        def _():
            relay(chips - 1 - k_up, False, has_below)

    mate_copy(chip).wait_recv()
    take(chip, mate_in)

    @pl.when(has_above)
    def _():
        chain_copy(chip, True).wait_recv()
        take(chip, down_in)

    @pl.when(has_below)
    def _():
        chain_copy(chip, False).wait_recv()
        take(chip, up_in)

    def finish(rows):
        weight_grad[rows, :] = acc[chip, rows, :]

    sweep(finish)
    for i, (src, tmp, dst) in enumerate(local_pairs):
        pltpu.make_async_copy(src, tmp, load_sem.at[i]).wait()
        pltpu.make_async_copy(tmp, dst, store_sem.at[i]).start()
    for src, dst, send_sem, recv_sem in exchanges:
        for p in peers:
            cols = pl.ds(pl.multiple_of(p * width, width), width)
            pltpu.make_async_remote_copy(
                src_ref=src.at[:, p], dst_ref=dst.at[:, :, cols],
                send_sem=send_sem.at[0], recv_sem=recv_sem.at[p],
                device_id=(dp, p), device_id_type=MESH,
            ).wait_recv()
    for copy in sends:
        copy.wait_send()

    for t in range(chips):
        mate_copy(t).wait_send()

        @pl.when(chip != t)
        def _():
            chain_copy(t, True).wait_send()

    for i, (_, tmp, dst) in enumerate(local_pairs):
        pltpu.make_async_copy(tmp, dst, store_sem.at[i]).wait()


def reduce_all(n_seq, n_dp, hid, pre_t, attn, qgrad):
    stretches, _, tokens, width = attn.shape
    chips = n_dp // CORES
    height = pre_t.shape[0]
    depth = hid.shape[1] // n_dp
    bf16, f32 = jnp.bfloat16, jnp.float32
    dma = pltpu.SemaphoreType.DMA
    out = (stretches, tokens, n_seq * width)
    own = (stretches, tokens, width)
    blocks = (chips, height, depth)
    return pl.pallas_call(
        functools.partial(reduce_kernel, n_seq, n_dp, math.gcd(depth, 256)),
        out_shape=[
            jax.ShapeDtypeStruct(out, bf16),
            jax.ShapeDtypeStruct(out, bf16),
            jax.ShapeDtypeStruct((height, depth), f32),
        ],
        in_specs=[VMEM, VMEM, ANY, ANY],
        out_specs=[ANY, ANY, VMEM],
        scratch_shapes=[
            pltpu.VMEM(own, bf16),
            pltpu.VMEM(own, bf16),
            pltpu.VMEM(blocks, f32),
            pltpu.VMEM(blocks, bf16),
            pltpu.VMEM(blocks, bf16),
            pltpu.VMEM(blocks, bf16),
            pltpu.VMEM(blocks, bf16),
            pltpu.VMEM(blocks, bf16),
            dma((2,)), dma((2,)),
            dma((n_seq,)), dma((n_seq,)), dma((n_seq,)), dma((n_seq,)),
            dma((chips,)), dma((chips,)), dma((chips,)), dma((chips,)), dma((chips,)),
        ],
        compiler_params=pltpu.CompilerParams(
            collective_id=1, has_side_effects=True, vmem_limit_bytes=VMEM_LIMIT
        ),
        name="reduce_all",
    )(hid, pre_t, attn, qgrad)


def local(n_seq, n_dp, hidden, queries, key_matrix, value_matrix, out_grad):
    hid, qry, grd, key_full, val_full = gather_all(
        n_seq, n_dp, hidden, queries, key_matrix, value_matrix, out_grad
    )
    stretches, _, tokens, width = qry.shape
    total = stretches * n_seq * tokens
    embed = hid.shape[-1]
    hid = hid.reshape(total, embed)
    kv_width = key_matrix.shape[1]
    f32 = jnp.float32
    key_raw = jnp.dot(hid, key_full.reshape(embed, kv_width), preferred_element_type=f32)
    val_raw = jnp.dot(hid, val_full.reshape(embed, kv_width), preferred_element_type=f32)
    attn, qgrad, pre_t = attention(
        key_raw, val_raw, qry.reshape(total, width), grd.reshape(total, width)
    )
    attn_out, query_grad, grad_t = reduce_all(
        n_seq, n_dp, hid, pre_t, attn.reshape(qry.shape), qgrad.reshape(qry.shape)
    )
    return attn_out[None], query_grad[None], grad_t[:kv_width].T, grad_t[kv_width:].T


def solution(mesh):
    n_dp, n_seq = mesh.shape["dp"], mesh.shape["seq"]
    tokens, weights = P("dp", None, "seq", None), P("dp", "seq")
    return jax.shard_map(
        functools.partial(local, n_seq, n_dp),
        mesh=mesh,
        in_specs=(tokens, tokens, weights, weights, tokens),
        out_specs=(tokens, tokens, weights, weights),
        check_vma=False,
    )
```

```python
import functools
import math

import jax
import jax.numpy as jnp
import numpy as np
from jax import lax
from jax.experimental import pallas as pl
from jax.experimental.pallas import tpu as pltpu
from jax.sharding import PartitionSpec as P

HEAD_WIDTH = 128
ROPE_BASE = 500000.0
CORES = 2
MESH = pl.DeviceIdType.MESH
ANY = pl.BlockSpec(memory_space=pl.ANY)
VMEM = pl.BlockSpec(memory_space=pltpu.VMEM)
VMEM_LIMIT = 63 << 20


def grid_of(count):
    rows = 2 if count % 2 == 0 else 1
    return rows, count // rows


def place(n_seq, n_dp):
    dp, seq = lax.axis_index("dp"), lax.axis_index("seq")
    chips = n_dp // CORES
    chip, core = lax.div(dp, CORES), lax.rem(dp, CORES)
    rows, cols = grid_of(n_seq)
    row, col = lax.div(seq, cols), lax.rem(seq, cols)
    row_peers = [row * cols + lax.rem(col + d, cols) for d in range(1, cols)]
    col_peers = [lax.rem(row + d, rows) * cols + col for d in range(1, rows)]
    far_peers = [
        lax.rem(row + e, rows) * cols + lax.rem(col + d, cols)
        for e in range(1, rows)
        for d in range(1, cols)
    ]
    return dp, seq, chips, chip, core, row_peers, col_peers, far_peers


def greet(dp, seq, chips, chip, core, peers):
    barrier = pltpu.get_barrier_semaphore()
    ids = [(dp, p) for p in peers]
    ids.append((chip * CORES + 1 - core, seq))
    if chips > 1:
        for d in (1, chips - 1):
            ids.append((lax.rem(chip + d, chips) * CORES + core, seq))
    for device in ids:
        pl.semaphore_signal(barrier, inc=1, device_id=device, device_id_type=MESH)
    pl.semaphore_wait(barrier, len(ids))


def kernel(
    n_seq, n_dp, kv_heads, group, tile,
    hidden, queries, key_matrix, value_matrix, out_grad, cos, sin, cos_t, sin_t,
    attn_out, qgrad_out, key_grad, val_grad,
    hid, qry, grd, key_all, val_all, key_raw, val_raw, keys, vals, attn, qgrad, pre_t,
    key_acc, val_acc, acc, mate_out, mate_in, chain_out, down_in, up_in,
    load_sem, own_sem, store_sem, hid_send, hid_recv, qry_send, qry_recv, grd_send, grd_recv,
    up_send, down_send, mate_w_send, w_recv, a_send, a_recv, q_send, q_recv,
    mate_send, mate_recv, chain_send, down_recv, up_recv,
):
    f32, bf16 = jnp.float32, jnp.bfloat16
    dp, seq, chips, chip, core, row_peers, col_peers, far_peers = place(n_seq, n_dp)
    peers = row_peers + col_peers + far_peers
    above, below = dp + CORES, dp - CORES
    mate = chip * CORES + 1 - core
    has_above, has_below = chip < chips - 1, chip > 0
    wide = group * HEAD_WIDTH
    width = kv_heads * wide
    total = keys.shape[0]
    half = HEAD_WIDTH // 2
    block = total // 2

    def head_cols(target, kv):
        return pl.ds(pl.multiple_of(target * width + kv * wide, wide), wide)

    loads = [
        (hidden, hid.at[:, seq], load_sem.at[0]),
        (key_matrix, key_all.at[dp], load_sem.at[1]),
        (value_matrix, val_all.at[dp], load_sem.at[2]),
    ]
    own_loads = []
    for kv in range(kv_heads):
        own_loads.append((
            (queries.at[:, :, head_cols(seq, kv)], qry.at[kv, :, seq], own_sem.at[0, kv]),
            (out_grad.at[:, :, head_cols(seq, kv)], grd.at[kv, :, seq], own_sem.at[1, kv]),
        ))
    greet(dp, seq, chips, chip, core, peers)
    sends = []
    slots = iter(range(hid_send.shape[0]))

    def send_hidden(source, part, target, src):
        copy = pltpu.make_async_remote_copy(
            src_ref=src, dst_ref=hid.at[part, source],
            send_sem=hid_send.at[next(slots)], recv_sem=hid_recv.at[source, part],
            device_id=(dp, target), device_id_type=MESH,
        )
        copy.start()
        sends.append(copy)

    def wait_hidden(source, part):
        pltpu.make_async_remote_copy(
            src_ref=hid.at[part, source], dst_ref=hid.at[part, source],
            send_sem=hid_send.at[0], recv_sem=hid_recv.at[source, part],
            device_id=(dp, source), device_id_type=MESH,
        ).wait_recv()

    tables = (key_all, val_all)
    owns = (key_matrix, value_matrix)

    def weight_copy(kind, piece, target_dp, send_sem, own=False):
        return pltpu.make_async_remote_copy(
            src_ref=owns[kind] if own else tables[kind].at[piece],
            dst_ref=tables[kind].at[piece],
            send_sem=send_sem, recv_sem=w_recv.at[piece, kind],
            device_id=(target_dp, seq), device_id_type=MESH,
        )

    def go(cond, copy_of, wait=False):
        @pl.when(cond)
        def _():
            copy = copy_of()
            copy.wait_send() if wait else copy.start()

    for p in row_peers:
        send_hidden(seq, 0, p, hidden.at[0])
    for p in col_peers:
        send_hidden(seq, 1, p, hidden.at[1])
    for kind in range(2):
        go(has_above, lambda: weight_copy(kind, dp, above, up_send.at[0, kind], True))
        go(has_below, lambda: weight_copy(kind, dp, below, down_send.at[0, kind], True))
    for p in row_peers:
        send_hidden(seq, 1, p, hidden.at[1])
    for p in col_peers:
        send_hidden(seq, 0, p, hidden.at[0])
    for kind in range(2):
        weight_copy(kind, dp, mate, mate_w_send.at[dp, kind], True).start()
    for copy in loads + [c for pair in own_loads for c in pair]:
        pltpu.make_async_copy(*copy).start()

    def relay_weight(step, kind):
        low, high = dp - CORES * step, dp + CORES * step

        @pl.when(chip >= step)
        def _():
            weight_copy(kind, low, below, up_send.at[step, kind]).wait_recv()
            go(has_above, lambda: weight_copy(kind, low, above, up_send.at[step, kind]))
            weight_copy(kind, low, mate, mate_w_send.at[low, kind]).start()

        @pl.when(chip + step < chips)
        def _():
            weight_copy(kind, high, above, down_send.at[step, kind]).wait_recv()
            go(has_below, lambda: weight_copy(kind, high, below, down_send.at[step, kind]))
            weight_copy(kind, high, mate, mate_w_send.at[high, kind]).start()

    def relay_hidden():
        for p in row_peers:
            wait_hidden(p, 0)
            for q in col_peers:
                send_hidden(p, 0, q, hid.at[0, p])
        for p in col_peers:
            wait_hidden(p, 1)
            for q in row_peers:
                send_hidden(p, 1, q, hid.at[1, p])

    def exchange(kv, src, dst, send_sem, recv_sem):
        for i, p in enumerate(peers):
            copy = pltpu.make_async_remote_copy(
                src_ref=src.at[:, :, head_cols(p, kv)], dst_ref=dst.at[kv, :, seq],
                send_sem=send_sem.at[kv, i], recv_sem=recv_sem.at[kv, seq],
                device_id=(dp, p), device_id_type=MESH,
            )
            copy.start()
            sends.append(copy)

    def wait_exchange(kv, dst, send_sem, recv_sem):
        for p in peers:
            pltpu.make_async_remote_copy(
                src_ref=dst.at[kv, :, p], dst_ref=dst.at[kv, :, p],
                send_sem=send_sem.at[kv, 0], recv_sem=recv_sem.at[kv, p],
                device_id=(dp, p), device_id_type=MESH,
            ).wait_recv()

    if chips > 1:
        relay_weight(1, 0)
    relay_hidden()
    for kv in range(kv_heads):
        exchange(kv, queries, qry, qry_send, qry_recv)
        exchange(kv, out_grad, grd, grd_send, grd_recv)
    if chips > 1:
        relay_weight(1, 1)
    for step in range(2, chips):
        for kind in range(2):
            relay_weight(step, kind)
    for p in row_peers:
        wait_hidden(p, 1)
    for p in col_peers:
        wait_hidden(p, 0)
    for p in far_peers:
        wait_hidden(p, 0)
        wait_hidden(p, 1)
    for other in range(chips):
        for kind in range(2):
            piece = other * CORES + 1 - core
            weight_copy(kind, piece, mate, mate_w_send.at[piece, kind]).wait_recv()
    for copy in loads:
        pltpu.make_async_copy(*copy).wait()

    key_raw[...] = jnp.zeros_like(key_raw)
    val_raw[...] = jnp.zeros_like(val_raw)
    deep = key_all.shape[1]

    @pl.loop(0, n_dp)
    def _(d):
        cols = pl.ds(pl.multiple_of(d * deep, deep), deep)
        rows = hid[:, :, :, cols].reshape(total, deep)
        key_raw[...] += jnp.dot(rows, key_all[d], preferred_element_type=f32)
        val_raw[...] += jnp.dot(rows, val_all[d], preferred_element_type=f32)

    for kv in range(kv_heads):
        lanes = pl.ds(kv * HEAD_WIDTH, HEAD_WIDTH)
        raw = key_raw[:, lanes]
        swapped = jnp.concatenate([raw[:, half:], raw[:, :half]], axis=1)
        keys[:, lanes] = (raw * cos[...] + swapped * sin[...]).astype(bf16)
    vals[...] = val_raw[...].astype(bf16)

    scale = 1.0 / math.sqrt(HEAD_WIDTH)
    nt = (((1,), (1,)), ((), ()))
    tn = (((0,), (0,)), ((), ()))

    def attend(kv):
        lanes = pl.ds(kv * HEAD_WIDTH, HEAD_WIDTH)
        key_acc[...] = jnp.zeros_like(key_acc)
        val_acc[...] = jnp.zeros_like(val_acc)

        @pl.loop(0, group)
        def _(m):
            head = pl.ds(pl.multiple_of(m * HEAD_WIDTH, HEAD_WIDTH), HEAD_WIDTH)
            for b in range(2):
                span = (b + 1) * block
                q = qry[kv, b, :, :, head].reshape(block, HEAD_WIDTH)
                g = grd[kv, b, :, :, head].reshape(block, HEAD_WIDTH)
                k, v = keys[:span, lanes], vals[:span, lanes]
                s = lax.dot_general(q, k, nt, preferred_element_type=f32) * scale
                at = b * block + lax.broadcasted_iota(jnp.int32, s.shape, 0)
                col = lax.broadcasted_iota(jnp.int32, s.shape, 1)
                s = jnp.where(col <= at, s, -jnp.inf)
                e = jnp.exp(s - jnp.max(s, axis=1, keepdims=True))
                p = e * (1.0 / jnp.sum(e, axis=1, keepdims=True))
                p_half = p.astype(bf16)
                o = jnp.dot(p_half, v, preferred_element_type=f32).astype(bf16)
                attn[kv, b, :, :, head] = o.reshape(n_seq, block // n_seq, HEAD_WIDTH)
                dot = jnp.sum(g.astype(f32) * o.astype(f32), axis=1, keepdims=True)
                gp = lax.dot_general(g, v, nt, preferred_element_type=f32)
                ds = (p * (gp - dot) * scale).astype(bf16)
                dq = jnp.dot(ds, k, preferred_element_type=f32).astype(bf16)
                qgrad[kv, b, :, :, head] = dq.reshape(n_seq, block // n_seq, HEAD_WIDTH)
                key_acc[:, :span] += lax.dot_general(q, ds, tn, preferred_element_type=f32)
                val_acc[:, :span] += lax.dot_general(g, p_half, tn, preferred_element_type=f32)

        grown = key_acc[...]
        swapped = jnp.concatenate([grown[half:, :], grown[:half, :]], axis=0)
        pre_t[kv, :HEAD_WIDTH, :] = (grown * cos_t[...] - swapped * sin_t[...]).astype(bf16)
        pre_t[kv, HEAD_WIDTH:, :] = val_acc[...].astype(bf16)

    height, depth = acc.shape[2], acc.shape[3]
    results = ((attn, attn_out, a_send, a_recv), (qgrad, qgrad_out, q_send, q_recv))

    def own_store(kv, which):
        src, dst, _, _ = results[which]
        return pltpu.make_async_copy(
            src.at[kv, :, seq], dst.at[:, :, head_cols(seq, kv)], store_sem.at[which, kv]
        )

    def give_back(kv):
        for which, (src, dst, send_sem, recv_sem) in enumerate(results):
            for i, p in enumerate(peers):
                copy = pltpu.make_async_remote_copy(
                    src_ref=src.at[kv, :, p], dst_ref=dst.at[:, :, head_cols(seq, kv)],
                    send_sem=send_sem.at[kv, i], recv_sem=recv_sem.at[kv, seq],
                    device_id=(dp, p), device_id_type=MESH,
                )
                copy.start()
                sends.append(copy)
            own_store(kv, which).start()

    def wait_back(kv):
        for which, (src, dst, send_sem, recv_sem) in enumerate(results):
            for p in peers:
                pltpu.make_async_remote_copy(
                    src_ref=src.at[kv, :, p], dst_ref=dst.at[:, :, head_cols(p, kv)],
                    send_sem=send_sem.at[kv, 0], recv_sem=recv_sem.at[kv, p],
                    device_id=(dp, p), device_id_type=MESH,
                ).wait_recv()
            own_store(kv, which).wait()

    def mate_copy(kv, t):
        return pltpu.make_async_remote_copy(
            src_ref=mate_out.at[kv, t], dst_ref=mate_in.at[kv, t],
            send_sem=mate_send.at[kv, t], recv_sem=mate_recv.at[kv, t],
            device_id=(mate, seq), device_id_type=MESH,
        )

    def chain_copy(kv, t, down):
        return pltpu.make_async_remote_copy(
            src_ref=chain_out.at[kv, t], dst_ref=(down_in if down else up_in).at[kv, t],
            send_sem=chain_send.at[kv, t], recv_sem=(down_recv if down else up_recv).at[kv, t],
            device_id=(below if down else above, seq), device_id_type=MESH,
        )

    def product(kv, which, store):
        @pl.loop(0, depth // tile)
        def _(i):
            cols = pl.ds(pl.multiple_of(which * depth + i * tile, tile), tile)
            rows = hid[:, :, :, cols].reshape(total, tile)
            part = jnp.dot(pre_t[kv], rows, preferred_element_type=f32)
            store(pl.ds(pl.multiple_of(i * tile, tile), tile), part)

    def products(kv):
        @pl.loop(0, chips)
        def _(i):
            odd, k = lax.rem(i, 2), lax.div(i, 2)
            t = odd * (chips - 1 - k) + (1 - odd) * k

            def to_mate(cols, part):
                mate_out[kv, t, :, cols] = part.astype(bf16)

            def to_acc(cols, part):
                acc[kv, t, :, cols] = part

            product(kv, t * CORES + 1 - core, to_mate)
            mate_copy(kv, t).start()
            product(kv, t * CORES + core, to_acc)

    strip = 32

    def sweep(fn):
        @pl.loop(0, height // strip)
        def _(i):
            fn(pl.ds(pl.multiple_of(i * strip, strip), strip))

    def relay(kv, t, down, has_input):
        mate_copy(kv, t).wait_recv()

        def merge(extra):
            def fn(rows):
                v = acc[kv, t, rows, :]
                for e in (mate_in,) + extra:
                    v = v + e[kv, t, rows, :].astype(f32)
                chain_out[kv, t, rows, :] = v.astype(bf16)

            sweep(fn)

        @pl.when(has_input)
        def _():
            chain_copy(kv, t, down).wait_recv()
            merge((down_in if down else up_in,))

        @pl.when(jnp.logical_not(has_input))
        def _():
            merge(())

        chain_copy(kv, t, down).start()

    is_end = jnp.logical_or(chip == 0, chip == chips - 1)

    def chain(kv, cond):
        @pl.when(cond)
        def _():
            @pl.loop(0, chips - 1)
            def _(tau):
                k_down = tau - (chips - 1 - chip)
                k_up = tau - chip

                @pl.when(jnp.logical_and(k_down >= 0, k_down < chip))
                def _():
                    relay(kv, k_down, True, has_above)

                @pl.when(jnp.logical_and(k_up >= 0, k_up < chips - 1 - chip))
                def _():
                    relay(kv, chips - 1 - k_up, False, has_below)

    def finish(kv):
        mate_copy(kv, chip).wait_recv()

        def take(extra):
            def fn(rows):
                acc[kv, chip, rows, :] += extra[kv, chip, rows, :].astype(f32)

            sweep(fn)

        take(mate_in)

        @pl.when(has_above)
        def _():
            chain_copy(kv, chip, True).wait_recv()
            take(down_in)

        @pl.when(has_below)
        def _():
            chain_copy(kv, chip, False).wait_recv()
            take(up_in)

        lanes = pl.ds(kv * HEAD_WIDTH, HEAD_WIDTH)

        @pl.loop(0, depth // HEAD_WIDTH)
        def _(j):
            at = pl.ds(pl.multiple_of(j * HEAD_WIDTH, HEAD_WIDTH), HEAD_WIDTH)
            key_grad[at, lanes] = acc[kv, chip, :HEAD_WIDTH, at].T
            val_grad[at, lanes] = acc[kv, chip, HEAD_WIDTH:, at].T

    last = kv_heads - 1
    for kv in range(kv_heads):
        wait_exchange(kv, qry, qry_send, qry_recv)
        wait_exchange(kv, grd, grd_send, grd_recv)
        for copy in own_loads[kv]:
            pltpu.make_async_copy(*copy).wait()
        attend(kv)
        products(kv)
        give_back(kv)
        if kv < last:
            chain(kv, is_end)
    for kv in range(kv_heads):
        chain(kv, jnp.logical_not(is_end) if kv < last else chip >= 0)
    for kv in range(kv_heads):
        finish(kv)
    for kv in range(kv_heads):
        wait_back(kv)
    for copy in sends:
        copy.wait_send()
    for kind in range(2):
        for step in range(max(chips - 1, 1)):
            low, high = dp - CORES * step, dp + CORES * step
            go(jnp.logical_and(has_above, chip >= step),
               lambda: weight_copy(kind, low, above, up_send.at[step, kind]), True)
            go(jnp.logical_and(has_below, chip + step < chips),
               lambda: weight_copy(kind, high, below, down_send.at[step, kind]), True)
        for other in range(chips):
            piece = other * CORES + core
            weight_copy(kind, piece, mate, mate_w_send.at[piece, kind]).wait_send()
    for kv in range(kv_heads):
        for t in range(chips):
            mate_copy(kv, t).wait_send()
            go(chip != t, lambda: chain_copy(kv, t, True), True)


def local(n_seq, n_dp, hidden, queries, key_matrix, value_matrix, out_grad):
    _, stretches, tokens, embed = hidden.shape
    full = queries.shape[3]
    width = full // n_seq
    deep, kv_width = key_matrix.shape
    kv_heads = kv_width // HEAD_WIDTH
    group = width // kv_width
    wide = group * HEAD_WIDTH
    chips = n_dp // CORES
    rows, cols = grid_of(n_seq)
    hid_sends = 2 * (rows - 1 + cols - 1) + 2 * (rows - 1) * (cols - 1)
    total = stretches * n_seq * tokens
    bf16, f32 = jnp.bfloat16, jnp.float32
    dma = pltpu.SemaphoreType.DMA
    half = HEAD_WIDTH // 2
    inverse = np.exp(
        np.arange(half, dtype=np.float32) * np.float32(-2.0 * math.log(ROPE_BASE) / HEAD_WIDTH)
    ).astype(np.float32)
    phase = np.arange(total, dtype=np.float32)[:, None] * inverse[None, :]
    cos_half, sin_half = np.cos(phase), np.sin(phase)
    cos = np.concatenate([cos_half, cos_half], axis=1).astype(np.float32)
    sin = np.concatenate([-sin_half, sin_half], axis=1).astype(np.float32)
    heads = (kv_heads, stretches, n_seq, tokens, wide)
    height = 2 * HEAD_WIDTH
    blocks = (kv_heads, chips, height, deep)
    weights = (n_dp, deep, kv_width)
    attn_out, query_grad, key_grad, val_grad = pl.pallas_call(
        functools.partial(kernel, n_seq, n_dp, kv_heads, group, math.gcd(deep, 256)),
        out_shape=[
            jax.ShapeDtypeStruct((stretches, tokens, full), bf16),
            jax.ShapeDtypeStruct((stretches, tokens, full), bf16),
            jax.ShapeDtypeStruct((deep, kv_width), f32),
            jax.ShapeDtypeStruct((deep, kv_width), f32),
        ],
        in_specs=[ANY] * 5 + [VMEM] * 4,
        out_specs=[ANY, ANY, VMEM, VMEM],
        scratch_shapes=[
            pltpu.VMEM((stretches, n_seq, tokens, embed), bf16),
            pltpu.VMEM(heads, bf16),
            pltpu.VMEM(heads, bf16),
            pltpu.VMEM(weights, bf16),
            pltpu.VMEM(weights, bf16),
            pltpu.VMEM((total, kv_width), f32),
            pltpu.VMEM((total, kv_width), f32),
            pltpu.VMEM((total, kv_width), bf16),
            pltpu.VMEM((total, kv_width), bf16),
            pltpu.VMEM(heads, bf16),
            pltpu.VMEM(heads, bf16),
            pltpu.VMEM((kv_heads, height, total), bf16),
            pltpu.VMEM((HEAD_WIDTH, total), f32),
            pltpu.VMEM((HEAD_WIDTH, total), f32),
            pltpu.VMEM(blocks, f32),
            pltpu.VMEM(blocks, bf16),
            pltpu.VMEM(blocks, bf16),
            pltpu.VMEM(blocks, bf16),
            pltpu.VMEM(blocks, bf16),
            pltpu.VMEM(blocks, bf16),
            dma((3,)), dma((2, kv_heads)), dma((2, kv_heads)),
            dma((hid_sends,)), dma((n_seq, 2)),
            dma((kv_heads, n_seq)), dma((kv_heads, n_seq)),
            dma((kv_heads, n_seq)), dma((kv_heads, n_seq)),
            dma((chips, 2)), dma((chips, 2)), dma((n_dp, 2)), dma((n_dp, 2)),
            dma((kv_heads, n_seq)), dma((kv_heads, n_seq)),
            dma((kv_heads, n_seq)), dma((kv_heads, n_seq)),
            dma((kv_heads, chips)), dma((kv_heads, chips)), dma((kv_heads, chips)),
            dma((kv_heads, chips)), dma((kv_heads, chips)),
        ],
        compiler_params=pltpu.CompilerParams(
            collective_id=0, has_side_effects=True, vmem_limit_bytes=VMEM_LIMIT
        ),
        name="attention_step",
    )(hidden[0], queries[0], key_matrix, value_matrix, out_grad[0],
      cos, sin, cos.T.copy(), sin.T.copy())
    return attn_out[None], query_grad[None], key_grad, val_grad


def solution(mesh):
    n_dp, n_seq = mesh.shape["dp"], mesh.shape["seq"]
    tokens, weights = P("dp", None, "seq", None), P("dp", "seq")
    return jax.shard_map(
        functools.partial(local, n_seq, n_dp),
        mesh=mesh,
        in_specs=(tokens, tokens, weights, weights, tokens),
        out_specs=(tokens, tokens, weights, weights),
        check_vma=False,
    )
```

```python
import functools
import math

import jax
import jax.numpy as jnp
import numpy as np
from jax import lax
from jax.experimental import pallas as pl
from jax.experimental.pallas import tpu as pltpu
from jax.sharding import PartitionSpec as P

HEAD_WIDTH = 128
ROPE_BASE = 500000.0
CORES = 2
MESH = pl.DeviceIdType.MESH
ANY = pl.BlockSpec(memory_space=pl.ANY)
VMEM = pl.BlockSpec(memory_space=pltpu.VMEM)
VMEM_LIMIT = 63 << 20


def grid_of(count):
    rows = 2 if count % 2 == 0 else 1
    return rows, count // rows


def place(n_seq, n_dp):
    dp, seq = lax.axis_index("dp"), lax.axis_index("seq")
    chips = n_dp // CORES
    chip, core = lax.div(dp, CORES), lax.rem(dp, CORES)
    rows, cols = grid_of(n_seq)
    row, col = lax.div(seq, cols), lax.rem(seq, cols)
    row_peers = [row * cols + lax.rem(col + d, cols) for d in range(1, cols)]
    col_peers = [lax.rem(row + d, rows) * cols + col for d in range(1, rows)]
    far_peers = [
        lax.rem(row + e, rows) * cols + lax.rem(col + d, cols)
        for e in range(1, rows)
        for d in range(1, cols)
    ]
    return dp, seq, chips, chip, core, row_peers, col_peers, far_peers


def greet(dp, seq, chips, chip, core, peers):
    barrier = pltpu.get_barrier_semaphore()
    ids = [(dp, p) for p in peers]
    ids.append((chip * CORES + 1 - core, seq))
    if chips > 1:
        for d in (1, chips - 1):
            ids.append((lax.rem(chip + d, chips) * CORES + core, seq))
    for device in ids:
        pl.semaphore_signal(barrier, inc=1, device_id=device, device_id_type=MESH)
    pl.semaphore_wait(barrier, len(ids))


def kernel(
    n_seq, n_dp, kv_heads, group, tile,
    hidden, queries, key_matrix, value_matrix, out_grad, cos, sin, cos_t, sin_t,
    attn_out, qgrad_out, key_grad, val_grad,
    hid, qry, grd, key_all, val_all, raw_both, keys, vals, attn, qgrad, pre_t,
    key_acc, val_acc, acc, mate_out, mate_in, chain_out, down_in, up_in,
    load_sem, own_sem, store_sem, hid_send, hid_recv, qry_send, qry_recv, grd_send, grd_recv,
    up_send, down_send, mate_w_send, w_recv, a_send, a_recv, q_send, q_recv,
    mate_send, mate_recv, chain_send, down_recv, up_recv,
):
    f32, bf16 = jnp.float32, jnp.bfloat16
    dp, seq, chips, chip, core, row_peers, col_peers, far_peers = place(n_seq, n_dp)
    peers = row_peers + col_peers + far_peers
    above, below = dp + CORES, dp - CORES
    mate = chip * CORES + 1 - core
    has_above, has_below = chip < chips - 1, chip > 0
    wide = group * HEAD_WIDTH
    width = kv_heads * wide
    total = keys.shape[0]
    half = HEAD_WIDTH // 2
    block = total // 2

    def head_cols(target, kv):
        return pl.ds(pl.multiple_of(target * width + kv * wide, wide), wide)

    def one_head(target, h):
        start = pl.multiple_of(target * width + h * HEAD_WIDTH, HEAD_WIDTH)
        return pl.ds(start, HEAD_WIDTH)

    loads = [
        (hidden, hid.at[:, seq], load_sem.at[0]),
        (key_matrix, key_all.at[dp], load_sem.at[1]),
        (value_matrix, val_all.at[dp], load_sem.at[2]),
    ]

    def own_loads(h):
        return (
            (queries.at[:, :, one_head(seq, h)], qry.at[h, :, seq], own_sem.at[0, h]),
            (out_grad.at[:, :, one_head(seq, h)], grd.at[h, :, seq], own_sem.at[1, h]),
        )

    greet(dp, seq, chips, chip, core, peers)
    sends = []
    slots = iter(range(hid_send.shape[0]))

    def send_hidden(source, part, target, src):
        copy = pltpu.make_async_remote_copy(
            src_ref=src, dst_ref=hid.at[part, source],
            send_sem=hid_send.at[next(slots)], recv_sem=hid_recv.at[source, part],
            device_id=(dp, target), device_id_type=MESH,
        )
        copy.start()
        sends.append(copy)

    def wait_hidden(source, part):
        pltpu.make_async_remote_copy(
            src_ref=hid.at[part, source], dst_ref=hid.at[part, source],
            send_sem=hid_send.at[0], recv_sem=hid_recv.at[source, part],
            device_id=(dp, source), device_id_type=MESH,
        ).wait_recv()

    tables = (key_all, val_all)
    owns = (key_matrix, value_matrix)

    def weight_copy(kind, piece, target_dp, send_sem, own=False):
        return pltpu.make_async_remote_copy(
            src_ref=owns[kind] if own else tables[kind].at[piece],
            dst_ref=tables[kind].at[piece],
            send_sem=send_sem, recv_sem=w_recv.at[piece, kind],
            device_id=(target_dp, seq), device_id_type=MESH,
        )

    def go(cond, copy_of, wait=False):
        @pl.when(cond)
        def _():
            copy = copy_of()
            copy.wait_send() if wait else copy.start()

    for p in row_peers:
        send_hidden(seq, 0, p, hidden.at[0])
    for p in col_peers:
        send_hidden(seq, 1, p, hidden.at[1])
    for kind in range(2):
        go(has_above, lambda: weight_copy(kind, dp, above, up_send.at[0, kind], True))
        go(has_below, lambda: weight_copy(kind, dp, below, down_send.at[0, kind], True))
    for p in row_peers:
        send_hidden(seq, 1, p, hidden.at[1])
    for p in col_peers:
        send_hidden(seq, 0, p, hidden.at[0])
    for kind in range(2):
        weight_copy(kind, dp, mate, mate_w_send.at[dp, kind], True).start()
    for copy in loads + [c for h in range(kv_heads * group) for c in own_loads(h)]:
        pltpu.make_async_copy(*copy).start()

    def relay_weight(step, kind):
        low, high = dp - CORES * step, dp + CORES * step

        @pl.when(chip >= step)
        def _():
            weight_copy(kind, low, below, up_send.at[step, kind]).wait_recv()
            go(has_above, lambda: weight_copy(kind, low, above, up_send.at[step, kind]))
            weight_copy(kind, low, mate, mate_w_send.at[low, kind]).start()

        @pl.when(chip + step < chips)
        def _():
            weight_copy(kind, high, above, down_send.at[step, kind]).wait_recv()
            go(has_below, lambda: weight_copy(kind, high, below, down_send.at[step, kind]))
            weight_copy(kind, high, mate, mate_w_send.at[high, kind]).start()

    def relay_hidden():
        for p in row_peers:
            wait_hidden(p, 0)
            for q in col_peers:
                send_hidden(p, 0, q, hid.at[0, p])
        for p in col_peers:
            wait_hidden(p, 1)
            for q in row_peers:
                send_hidden(p, 1, q, hid.at[1, p])

    def exchange(h, src, dst, send_sem, recv_sem):
        for i, p in enumerate(peers):
            copy = pltpu.make_async_remote_copy(
                src_ref=src.at[:, :, one_head(p, h)], dst_ref=dst.at[h, :, seq],
                send_sem=send_sem.at[h, i], recv_sem=recv_sem.at[h, seq],
                device_id=(dp, p), device_id_type=MESH,
            )
            copy.start()
            sends.append(copy)

    def wait_exchange(h, dst, send_sem, recv_sem):
        for p in peers:
            pltpu.make_async_remote_copy(
                src_ref=dst.at[h, :, p], dst_ref=dst.at[h, :, p],
                send_sem=send_sem.at[h, 0], recv_sem=recv_sem.at[h, p],
                device_id=(dp, p), device_id_type=MESH,
            ).wait_recv()

    if chips > 1:
        relay_weight(1, 0)
    relay_hidden()
    for h in range(kv_heads * group):
        exchange(h, queries, qry, qry_send, qry_recv)
        exchange(h, out_grad, grd, grd_send, grd_recv)
    if chips > 1:
        relay_weight(1, 1)
    for step in range(2, chips):
        for kind in range(2):
            relay_weight(step, kind)
    for p in row_peers:
        wait_hidden(p, 1)
    for p in col_peers:
        wait_hidden(p, 0)
    for p in far_peers:
        wait_hidden(p, 0)
        wait_hidden(p, 1)
    for other in range(chips):
        for kind in range(2):
            piece = other * CORES + 1 - core
            weight_copy(kind, piece, mate, mate_w_send.at[piece, kind]).wait_recv()
    for copy in loads:
        pltpu.make_async_copy(*copy).wait()

    deep = key_all.shape[1]

    def project(kv):
        lanes = pl.ds(kv * HEAD_WIDTH, HEAD_WIDTH)
        raw_both[...] = jnp.zeros_like(raw_both)

        @pl.loop(0, n_dp)
        def _(d):
            cols = pl.ds(pl.multiple_of(d * deep, deep), deep)
            rows = hid[:, :, :, cols].reshape(total, deep)
            both = jnp.concatenate([key_all[d, :, lanes], val_all[d, :, lanes]], axis=1)
            raw_both[...] += jnp.dot(rows, both, preferred_element_type=f32)

        raw = raw_both[:, :HEAD_WIDTH]
        swapped = jnp.concatenate([raw[:, half:], raw[:, :half]], axis=1)
        keys[:, lanes] = (raw * cos[...] + swapped * sin[...]).astype(bf16)
        vals[:, lanes] = raw_both[:, HEAD_WIDTH:].astype(bf16)

    scale = 1.0 / math.sqrt(HEAD_WIDTH)
    nt = (((1,), (1,)), ((), ()))
    tn = (((0,), (0,)), ((), ()))

    def attend(kv):
        lanes = pl.ds(kv * HEAD_WIDTH, HEAD_WIDTH)
        key_acc[...] = jnp.zeros_like(key_acc)
        val_acc[...] = jnp.zeros_like(val_acc)

        @pl.loop(0, group)
        def _(m):
            head = pl.ds(pl.multiple_of(m * HEAD_WIDTH, HEAD_WIDTH), HEAD_WIDTH)
            h = kv * group + m
            wait_exchange(h, qry, qry_send, qry_recv)
            wait_exchange(h, grd, grd_send, grd_recv)
            for copy in own_loads(h):
                pltpu.make_async_copy(*copy).wait()
            for b in range(2):
                span = (b + 1) * block
                q = qry[h, b].reshape(block, HEAD_WIDTH)
                g = grd[h, b].reshape(block, HEAD_WIDTH)
                k, v = keys[:span, lanes], vals[:span, lanes]
                s = lax.dot_general(q, k, nt, preferred_element_type=f32) * scale
                at = b * block + lax.broadcasted_iota(jnp.int32, s.shape, 0)
                col = lax.broadcasted_iota(jnp.int32, s.shape, 1)
                s = jnp.where(col <= at, s, -jnp.inf)
                e = jnp.exp(s - jnp.max(s, axis=1, keepdims=True))
                p = e * (1.0 / jnp.sum(e, axis=1, keepdims=True))
                p_half = p.astype(bf16)
                o = jnp.dot(p_half, v, preferred_element_type=f32).astype(bf16)
                attn[kv, b, :, :, head] = o.reshape(n_seq, block // n_seq, HEAD_WIDTH)
                dot = jnp.sum(g.astype(f32) * o.astype(f32), axis=1, keepdims=True)
                gp = lax.dot_general(g, v, nt, preferred_element_type=f32)
                ds = (p * (gp - dot) * scale).astype(bf16)
                dq = jnp.dot(ds, k, preferred_element_type=f32).astype(bf16)
                qgrad[kv, b, :, :, head] = dq.reshape(n_seq, block // n_seq, HEAD_WIDTH)
                key_acc[:, :span] += lax.dot_general(q, ds, tn, preferred_element_type=f32)
                val_acc[:, :span] += lax.dot_general(g, p_half, tn, preferred_element_type=f32)

        grown = key_acc[...]
        swapped = jnp.concatenate([grown[half:, :], grown[:half, :]], axis=0)
        pre_t[kv, :HEAD_WIDTH, :] = (grown * cos_t[...] - swapped * sin_t[...]).astype(bf16)
        pre_t[kv, HEAD_WIDTH:, :] = val_acc[...].astype(bf16)

    height, depth = acc.shape[2], acc.shape[3]
    results = ((attn, attn_out, a_send, a_recv), (qgrad, qgrad_out, q_send, q_recv))

    def own_store(kv, which):
        src, dst, _, _ = results[which]
        return pltpu.make_async_copy(
            src.at[kv, :, seq], dst.at[:, :, head_cols(seq, kv)], store_sem.at[which, kv]
        )

    def give_back(kv):
        for which, (src, dst, send_sem, recv_sem) in enumerate(results):
            for i, p in enumerate(peers):
                copy = pltpu.make_async_remote_copy(
                    src_ref=src.at[kv, :, p], dst_ref=dst.at[:, :, head_cols(seq, kv)],
                    send_sem=send_sem.at[kv, i], recv_sem=recv_sem.at[kv, seq],
                    device_id=(dp, p), device_id_type=MESH,
                )
                copy.start()
                sends.append(copy)
            own_store(kv, which).start()

    def wait_back(kv):
        for which, (src, dst, send_sem, recv_sem) in enumerate(results):
            for p in peers:
                pltpu.make_async_remote_copy(
                    src_ref=src.at[kv, :, p], dst_ref=dst.at[:, :, head_cols(p, kv)],
                    send_sem=send_sem.at[kv, 0], recv_sem=recv_sem.at[kv, p],
                    device_id=(dp, p), device_id_type=MESH,
                ).wait_recv()
            own_store(kv, which).wait()

    def mate_copy(kv, t):
        return pltpu.make_async_remote_copy(
            src_ref=mate_out.at[kv, t], dst_ref=mate_in.at[kv, t],
            send_sem=mate_send.at[kv, t], recv_sem=mate_recv.at[kv, t],
            device_id=(mate, seq), device_id_type=MESH,
        )

    def chain_copy(kv, t, down):
        return pltpu.make_async_remote_copy(
            src_ref=chain_out.at[kv, t], dst_ref=(down_in if down else up_in).at[kv, t],
            send_sem=chain_send.at[kv, t], recv_sem=(down_recv if down else up_recv).at[kv, t],
            device_id=(below if down else above, seq), device_id_type=MESH,
        )

    def product(kv, which, store):
        @pl.loop(0, depth // tile)
        def _(i):
            cols = pl.ds(pl.multiple_of(which * depth + i * tile, tile), tile)
            rows = hid[:, :, :, cols].reshape(total, tile)
            part = jnp.dot(pre_t[kv], rows, preferred_element_type=f32)
            store(pl.ds(pl.multiple_of(i * tile, tile), tile), part)

    strip = 32

    def sweep(fn):
        @pl.loop(0, height // strip)
        def _(i):
            fn(pl.ds(pl.multiple_of(i * strip, strip), strip))

    def relay(kv, t, down, has_input):
        mate_copy(kv, t).wait_recv()

        def merge(extra):
            def fn(rows):
                v = acc[kv, t, rows, :]
                for e in (mate_in,) + extra:
                    v = v + e[kv, t, rows, :].astype(f32)
                chain_out[kv, t, rows, :] = v.astype(bf16)

            sweep(fn)

        if has_input:
            chain_copy(kv, t, down).wait_recv()
            merge((down_in if down else up_in,))
        else:
            merge(())
        chain_copy(kv, t, down).start()

    is_end = jnp.logical_or(chip == 0, chip == chips - 1)

    flip = lax.div(chips - 1 - chip, max(chips - 1, 1)) if chips > 1 else 0

    def turn(i):
        odd, k = lax.rem(i, 2), lax.div(i, 2)
        t = odd * (chips - 1 - k) + (1 - odd) * k
        return flip * (chips - 1 - t) + (1 - flip) * t

    def early(kv, t):
        @pl.when(jnp.logical_and(chip == chips - 1, t < chip))
        def _():
            relay(kv, t, True, False)

        @pl.when(jnp.logical_and(chip == 0, t > chip))
        def _():
            relay(kv, t, False, False)

    def products(kv):
        @pl.loop(0, chips)
        def _(i):
            t = turn(i)

            def to_mate(cols, part):
                mate_out[kv, t, :, cols] = part.astype(bf16)

            def to_acc(cols, part):
                acc[kv, t, :, cols] = part

            product(kv, t * CORES + 1 - core, to_mate)
            mate_copy(kv, t).start()
            product(kv, t * CORES + core, to_acc)

            @pl.when(i > 0)
            def _():
                early(kv, turn(i - 1))

        early(kv, turn(chips - 1))

    def chain(kv, cond):
        @pl.when(cond)
        def _():
            @pl.loop(0, chips - 1)
            def _(tau):
                k_down = tau - (chips - 1 - chip)
                k_up = tau - chip

                @pl.when(jnp.logical_and(k_down >= 0, k_down < chip))
                def _():
                    relay(kv, k_down, True, True)

                @pl.when(jnp.logical_and(k_up >= 0, k_up < chips - 1 - chip))
                def _():
                    relay(kv, chips - 1 - k_up, False, True)

    def prepare(kv):
        mate_copy(kv, chip).wait_recv()

        def fn(rows):
            acc[kv, chip, rows, :] += mate_in[kv, chip, rows, :].astype(f32)

        sweep(fn)

    def finish(kv):
        lanes = pl.ds(kv * HEAD_WIDTH, HEAD_WIDTH)

        def put(extra):
            @pl.loop(0, depth // HEAD_WIDTH)
            def _(j):
                at = pl.ds(pl.multiple_of(j * HEAD_WIDTH, HEAD_WIDTH), HEAD_WIDTH)
                v = acc[kv, chip, :, at]
                for e in extra:
                    v = v + e[kv, chip, :, at].astype(f32)
                key_grad[at, lanes] = v[:HEAD_WIDTH, :].T
                val_grad[at, lanes] = v[HEAD_WIDTH:, :].T

        if chips == 1:
            put(())
            return

        @pl.when(has_above)
        def _():
            chain_copy(kv, chip, True).wait_recv()

        @pl.when(has_below)
        def _():
            chain_copy(kv, chip, False).wait_recv()

        @pl.when(chip == 0)
        def _():
            put((down_in,))

        @pl.when(chip == chips - 1)
        def _():
            put((up_in,))

        @pl.when(jnp.logical_not(is_end))
        def _():
            put((down_in, up_in))

    for kv in range(kv_heads):
        project(kv)
        attend(kv)
        products(kv)
        give_back(kv)
    for kv in range(kv_heads):
        prepare(kv)
        chain(kv, jnp.logical_not(is_end))
    for kv in range(kv_heads):
        wait_back(kv)
        finish(kv)
    for copy in sends:
        copy.wait_send()
    for kind in range(2):
        for step in range(max(chips - 1, 1)):
            low, high = dp - CORES * step, dp + CORES * step
            go(jnp.logical_and(has_above, chip >= step),
               lambda: weight_copy(kind, low, above, up_send.at[step, kind]), True)
            go(jnp.logical_and(has_below, chip + step < chips),
               lambda: weight_copy(kind, high, below, down_send.at[step, kind]), True)
        for other in range(chips):
            piece = other * CORES + core
            weight_copy(kind, piece, mate, mate_w_send.at[piece, kind]).wait_send()
    for kv in range(kv_heads):
        for t in range(chips):
            mate_copy(kv, t).wait_send()
            go(chip != t, lambda: chain_copy(kv, t, True), True)


def local(n_seq, n_dp, hidden, queries, key_matrix, value_matrix, out_grad):
    _, stretches, tokens, embed = hidden.shape
    full = queries.shape[3]
    width = full // n_seq
    deep, kv_width = key_matrix.shape
    kv_heads = kv_width // HEAD_WIDTH
    group = width // kv_width
    wide = group * HEAD_WIDTH
    chips = n_dp // CORES
    rows, cols = grid_of(n_seq)
    hid_sends = 2 * (rows - 1 + cols - 1) + 2 * (rows - 1) * (cols - 1)
    total = stretches * n_seq * tokens
    bf16, f32 = jnp.bfloat16, jnp.float32
    dma = pltpu.SemaphoreType.DMA
    half = HEAD_WIDTH // 2
    inverse = np.exp(
        np.arange(half, dtype=np.float32) * np.float32(-2.0 * math.log(ROPE_BASE) / HEAD_WIDTH)
    ).astype(np.float32)
    phase = np.arange(total, dtype=np.float32)[:, None] * inverse[None, :]
    cos_half, sin_half = np.cos(phase), np.sin(phase)
    cos = np.concatenate([cos_half, cos_half], axis=1).astype(np.float32)
    sin = np.concatenate([-sin_half, sin_half], axis=1).astype(np.float32)
    heads = (kv_heads, stretches, n_seq, tokens, wide)
    single = (kv_heads * group, stretches, n_seq, tokens, HEAD_WIDTH)
    height = 2 * HEAD_WIDTH
    blocks = (kv_heads, chips, height, deep)
    weights = (n_dp, deep, kv_width)
    attn_out, query_grad, key_grad, val_grad = pl.pallas_call(
        functools.partial(kernel, n_seq, n_dp, kv_heads, group, math.gcd(deep, 256)),
        out_shape=[
            jax.ShapeDtypeStruct((stretches, tokens, full), bf16),
            jax.ShapeDtypeStruct((stretches, tokens, full), bf16),
            jax.ShapeDtypeStruct((deep, kv_width), f32),
            jax.ShapeDtypeStruct((deep, kv_width), f32),
        ],
        in_specs=[ANY] * 5 + [VMEM] * 4,
        out_specs=[ANY, ANY, VMEM, VMEM],
        scratch_shapes=[
            pltpu.VMEM((stretches, n_seq, tokens, embed), bf16),
            pltpu.VMEM(single, bf16),
            pltpu.VMEM(single, bf16),
            pltpu.VMEM(weights, bf16),
            pltpu.VMEM(weights, bf16),
            pltpu.VMEM((total, 2 * HEAD_WIDTH), f32),
            pltpu.VMEM((total, kv_width), bf16),
            pltpu.VMEM((total, kv_width), bf16),
            pltpu.VMEM(heads, bf16),
            pltpu.VMEM(heads, bf16),
            pltpu.VMEM((kv_heads, height, total), bf16),
            pltpu.VMEM((HEAD_WIDTH, total), f32),
            pltpu.VMEM((HEAD_WIDTH, total), f32),
            pltpu.VMEM(blocks, f32),
            pltpu.VMEM(blocks, bf16),
            pltpu.VMEM(blocks, bf16),
            pltpu.VMEM(blocks, bf16),
            pltpu.VMEM(blocks, bf16),
            pltpu.VMEM(blocks, bf16),
            dma((3,)), dma((2, kv_heads * group)), dma((2, kv_heads)),
            dma((hid_sends,)), dma((n_seq, 2)),
            dma((kv_heads * group, n_seq)), dma((kv_heads * group, n_seq)),
            dma((kv_heads * group, n_seq)), dma((kv_heads * group, n_seq)),
            dma((chips, 2)), dma((chips, 2)), dma((n_dp, 2)), dma((n_dp, 2)),
            dma((kv_heads, n_seq)), dma((kv_heads, n_seq)),
            dma((kv_heads, n_seq)), dma((kv_heads, n_seq)),
            dma((kv_heads, chips)), dma((kv_heads, chips)), dma((kv_heads, chips)),
            dma((kv_heads, chips)), dma((kv_heads, chips)),
        ],
        compiler_params=pltpu.CompilerParams(
            collective_id=0, has_side_effects=True, vmem_limit_bytes=VMEM_LIMIT
        ),
        name="attention_step",
    )(hidden[0], queries[0], key_matrix, value_matrix, out_grad[0],
      cos, sin, cos.T.copy(), sin.T.copy())
    return attn_out[None], query_grad[None], key_grad, val_grad


def solution(mesh):
    n_dp, n_seq = mesh.shape["dp"], mesh.shape["seq"]
    tokens, weights = P("dp", None, "seq", None), P("dp", "seq")
    return jax.shard_map(
        functools.partial(local, n_seq, n_dp),
        mesh=mesh,
        in_specs=(tokens, tokens, weights, weights, tokens),
        out_specs=(tokens, tokens, weights, weights),
        check_vma=False,
    )
```

```python
import functools
import math

import jax
import jax.numpy as jnp
import numpy as np
from jax import lax
from jax.experimental import pallas as pl
from jax.experimental.pallas import tpu as pltpu
from jax.sharding import PartitionSpec as P

HEAD_WIDTH = 128
ROPE_BASE = 500000.0
CORES = 2
MESH = pl.DeviceIdType.MESH
ANY = pl.BlockSpec(memory_space=pl.ANY)
VMEM = pl.BlockSpec(memory_space=pltpu.VMEM)
VMEM_LIMIT = 56 << 20


def grid_of(count):
    rows = 2 if count % 2 == 0 else 1
    return rows, count // rows


def place(n_seq, n_dp):
    dp, seq = lax.axis_index("dp"), lax.axis_index("seq")
    chips = n_dp // CORES
    chip, core = lax.div(dp, CORES), lax.rem(dp, CORES)
    rows, cols = grid_of(n_seq)
    row, col = lax.div(seq, cols), lax.rem(seq, cols)
    row_peers = [row * cols + lax.rem(col + d, cols) for d in range(1, cols)]
    col_peers = [lax.rem(row + d, rows) * cols + col for d in range(1, rows)]
    far_peers = [
        lax.rem(row + e, rows) * cols + lax.rem(col + d, cols)
        for e in range(1, rows)
        for d in range(1, cols)
    ]
    return dp, seq, chips, chip, core, row_peers, col_peers, far_peers


def greet(dp, seq, chips, chip, core, peers):
    barrier = pltpu.get_barrier_semaphore()
    ids = [(dp, p) for p in peers]
    ids.append((chip * CORES + 1 - core, seq))
    if chips > 1:
        for d in (1, chips - 1):
            ids.append((lax.rem(chip + d, chips) * CORES + core, seq))
    for device in ids:
        pl.semaphore_signal(barrier, inc=1, device_id=device, device_id_type=MESH)
    pl.semaphore_wait(barrier, len(ids))


def kernel(
    n_seq, n_dp, kv_heads, group, tile,
    hidden, queries, key_matrix, value_matrix, out_grad, cos, sin, cos_t, sin_t,
    attn_out, qgrad_out, key_grad, val_grad,
    hid, qry, grd, key_all, val_all, raw_both, keys, vals, attn, qgrad, pre_t,
    key_acc, val_acc, acc, mate_out, mate_in, chain_out, down_in, up_in,
    load_sem, own_sem, store_sem, hid_send, hid_recv, qry_send, qry_recv, grd_send, grd_recv,
    up_send, down_send, mate_w_send, w_recv, a_send, a_recv, q_send, q_recv,
    mate_send, mate_recv, chain_send, down_recv, up_recv,
):
    f32, bf16 = jnp.float32, jnp.bfloat16
    dp, seq, chips, chip, core, row_peers, col_peers, far_peers = place(n_seq, n_dp)
    peers = row_peers + col_peers + far_peers
    above, below = dp + CORES, dp - CORES
    mate = chip * CORES + 1 - core
    has_above, has_below = chip < chips - 1, chip > 0
    wide = group * HEAD_WIDTH
    width = kv_heads * wide
    total = keys.shape[0]
    half = HEAD_WIDTH // 2
    block = total // 2

    def head_cols(target, kv):
        return pl.ds(pl.multiple_of(target * width + kv * wide, wide), wide)

    def one_head(target, h):
        start = pl.multiple_of(target * width + h * HEAD_WIDTH, HEAD_WIDTH)
        return pl.ds(start, HEAD_WIDTH)

    loads = [
        (hidden, hid.at[:, seq], load_sem.at[0]),
        (key_matrix, key_all.at[dp], load_sem.at[1]),
        (value_matrix, val_all.at[dp], load_sem.at[2]),
    ]

    def own_loads(h):
        return (
            (queries.at[:, :, one_head(seq, h)], qry.at[h, :, seq], own_sem.at[0, h]),
            (out_grad.at[:, :, one_head(seq, h)], grd.at[h, :, seq], own_sem.at[1, h]),
        )

    greet(dp, seq, chips, chip, core, peers)
    sends = []
    slots = iter(range(hid_send.shape[0]))

    def send_hidden(source, part, target, src):
        copy = pltpu.make_async_remote_copy(
            src_ref=src, dst_ref=hid.at[part, source],
            send_sem=hid_send.at[next(slots)], recv_sem=hid_recv.at[source, part],
            device_id=(dp, target), device_id_type=MESH,
        )
        copy.start()
        sends.append(copy)

    def wait_hidden(source, part):
        pltpu.make_async_remote_copy(
            src_ref=hid.at[part, source], dst_ref=hid.at[part, source],
            send_sem=hid_send.at[0], recv_sem=hid_recv.at[source, part],
            device_id=(dp, source), device_id_type=MESH,
        ).wait_recv()

    tables = (key_all, val_all)
    owns = (key_matrix, value_matrix)

    def weight_copy(kind, piece, target_dp, send_sem, own=False):
        return pltpu.make_async_remote_copy(
            src_ref=owns[kind] if own else tables[kind].at[piece],
            dst_ref=tables[kind].at[piece],
            send_sem=send_sem, recv_sem=w_recv.at[piece, kind],
            device_id=(target_dp, seq), device_id_type=MESH,
        )

    def go(cond, copy_of, wait=False):
        @pl.when(cond)
        def _():
            copy = copy_of()
            copy.wait_send() if wait else copy.start()

    for p in row_peers:
        send_hidden(seq, 0, p, hidden.at[0])
    for p in col_peers:
        send_hidden(seq, 1, p, hidden.at[1])
    for kind in range(2):
        go(has_above, lambda: weight_copy(kind, dp, above, up_send.at[0, kind], True))
        go(has_below, lambda: weight_copy(kind, dp, below, down_send.at[0, kind], True))
    for p in row_peers:
        send_hidden(seq, 1, p, hidden.at[1])
    for p in col_peers:
        send_hidden(seq, 0, p, hidden.at[0])
    for kind in range(2):
        weight_copy(kind, dp, mate, mate_w_send.at[dp, kind], True).start()
    for copy in loads + [c for h in range(kv_heads * group) for c in own_loads(h)]:
        pltpu.make_async_copy(*copy).start()

    def relay_weight(step, kind):
        low, high = dp - CORES * step, dp + CORES * step

        @pl.when(chip >= step)
        def _():
            weight_copy(kind, low, below, up_send.at[step, kind]).wait_recv()
            go(has_above, lambda: weight_copy(kind, low, above, up_send.at[step, kind]))
            weight_copy(kind, low, mate, mate_w_send.at[low, kind]).start()

        @pl.when(chip + step < chips)
        def _():
            weight_copy(kind, high, above, down_send.at[step, kind]).wait_recv()
            go(has_below, lambda: weight_copy(kind, high, below, down_send.at[step, kind]))
            weight_copy(kind, high, mate, mate_w_send.at[high, kind]).start()

    def relay_hidden():
        for p in row_peers:
            wait_hidden(p, 0)
            for q in col_peers:
                send_hidden(p, 0, q, hid.at[0, p])
        for p in col_peers:
            wait_hidden(p, 1)
            for q in row_peers:
                send_hidden(p, 1, q, hid.at[1, p])

    def exchange(h, src, dst, send_sem, recv_sem):
        for i, p in enumerate(peers):
            copy = pltpu.make_async_remote_copy(
                src_ref=src.at[:, :, one_head(p, h)], dst_ref=dst.at[h, :, seq],
                send_sem=send_sem.at[h, i], recv_sem=recv_sem.at[h, seq],
                device_id=(dp, p), device_id_type=MESH,
            )
            copy.start()
            sends.append(copy)

    def wait_exchange(h, dst, send_sem, recv_sem):
        for p in peers:
            pltpu.make_async_remote_copy(
                src_ref=dst.at[h, :, p], dst_ref=dst.at[h, :, p],
                send_sem=send_sem.at[h, 0], recv_sem=recv_sem.at[h, p],
                device_id=(dp, p), device_id_type=MESH,
            ).wait_recv()

    if chips > 1:
        relay_weight(1, 0)
    relay_hidden()
    for h in range(kv_heads * group):
        exchange(h, queries, qry, qry_send, qry_recv)
        exchange(h, out_grad, grd, grd_send, grd_recv)
    if chips > 1:
        relay_weight(1, 1)
    for step in range(2, chips):
        for kind in range(2):
            relay_weight(step, kind)
    for p in row_peers:
        wait_hidden(p, 1)
    for p in col_peers:
        wait_hidden(p, 0)
    for p in far_peers:
        wait_hidden(p, 0)
        wait_hidden(p, 1)
    for other in range(chips):
        for kind in range(2):
            piece = other * CORES + 1 - core
            weight_copy(kind, piece, mate, mate_w_send.at[piece, kind]).wait_recv()
    for copy in loads:
        pltpu.make_async_copy(*copy).wait()

    deep = key_all.shape[1]

    def project(kv):
        lanes = pl.ds(kv * HEAD_WIDTH, HEAD_WIDTH)
        raw_both[...] = jnp.zeros_like(raw_both)

        @pl.loop(0, n_dp)
        def _(d):
            cols = pl.ds(pl.multiple_of(d * deep, deep), deep)
            rows = hid[:, :, :, cols].reshape(total, deep)
            both = jnp.concatenate([key_all[d, :, lanes], val_all[d, :, lanes]], axis=1)
            raw_both[...] += jnp.dot(rows, both, preferred_element_type=f32)

        raw = raw_both[:, :HEAD_WIDTH]
        swapped = jnp.concatenate([raw[:, half:], raw[:, :half]], axis=1)
        keys[:, lanes] = (raw * cos[...] + swapped * sin[...]).astype(bf16)
        vals[:, lanes] = raw_both[:, HEAD_WIDTH:].astype(bf16)

    scale = 1.0 / math.sqrt(HEAD_WIDTH)
    nt = (((1,), (1,)), ((), ()))
    tn = (((0,), (0,)), ((), ()))

    def attend(kv):
        lanes = pl.ds(kv * HEAD_WIDTH, HEAD_WIDTH)
        key_acc[...] = jnp.zeros_like(key_acc)
        val_acc[...] = jnp.zeros_like(val_acc)

        @pl.loop(0, group)
        def _(m):
            head = pl.ds(pl.multiple_of(m * HEAD_WIDTH, HEAD_WIDTH), HEAD_WIDTH)
            h = kv * group + m
            wait_exchange(h, qry, qry_send, qry_recv)
            wait_exchange(h, grd, grd_send, grd_recv)
            for copy in own_loads(h):
                pltpu.make_async_copy(*copy).wait()
            for b in range(2):
                span = (b + 1) * block
                q = qry[h, b].reshape(block, HEAD_WIDTH)
                g = grd[h, b].reshape(block, HEAD_WIDTH)
                k, v = keys[:span, lanes], vals[:span, lanes]
                s = lax.dot_general(q, k, nt, preferred_element_type=f32) * scale
                at = b * block + lax.broadcasted_iota(jnp.int32, s.shape, 0)
                col = lax.broadcasted_iota(jnp.int32, s.shape, 1)
                s = jnp.where(col <= at, s, -jnp.inf)
                e = jnp.exp(s - jnp.max(s, axis=1, keepdims=True))
                p = e * (1.0 / jnp.sum(e, axis=1, keepdims=True))
                p_half = p.astype(bf16)
                o = jnp.dot(p_half, v, preferred_element_type=f32).astype(bf16)
                attn[kv, b, :, :, head] = o.reshape(n_seq, block // n_seq, HEAD_WIDTH)
                dot = jnp.sum(g.astype(f32) * o.astype(f32), axis=1, keepdims=True)
                gp = lax.dot_general(g, v, nt, preferred_element_type=f32)
                ds = (p * (gp - dot) * scale).astype(bf16)
                dq = jnp.dot(ds, k, preferred_element_type=f32).astype(bf16)
                qgrad[kv, b, :, :, head] = dq.reshape(n_seq, block // n_seq, HEAD_WIDTH)
                key_acc[:, :span] += lax.dot_general(q, ds, tn, preferred_element_type=f32)
                val_acc[:, :span] += lax.dot_general(g, p_half, tn, preferred_element_type=f32)

        grown = key_acc[...]
        swapped = jnp.concatenate([grown[half:, :], grown[:half, :]], axis=0)
        pre_t[kv, :HEAD_WIDTH, :] = (grown * cos_t[...] - swapped * sin_t[...]).astype(bf16)
        pre_t[kv, HEAD_WIDTH:, :] = val_acc[...].astype(bf16)

    height, depth = acc.shape[2], acc.shape[3]
    results = ((attn, attn_out, a_send, a_recv), (qgrad, qgrad_out, q_send, q_recv))

    def own_store(kv, which):
        src, dst, _, _ = results[which]
        return pltpu.make_async_copy(
            src.at[kv, :, seq], dst.at[:, :, head_cols(seq, kv)], store_sem.at[which, kv]
        )

    def give_back(kv):
        for which, (src, dst, send_sem, recv_sem) in enumerate(results):
            for i, p in enumerate(peers):
                copy = pltpu.make_async_remote_copy(
                    src_ref=src.at[kv, :, p], dst_ref=dst.at[:, :, head_cols(seq, kv)],
                    send_sem=send_sem.at[kv, i], recv_sem=recv_sem.at[kv, seq],
                    device_id=(dp, p), device_id_type=MESH,
                )
                copy.start()
                sends.append(copy)
            own_store(kv, which).start()

    def wait_back(kv):
        for which, (src, dst, send_sem, recv_sem) in enumerate(results):
            for p in peers:
                pltpu.make_async_remote_copy(
                    src_ref=src.at[kv, :, p], dst_ref=dst.at[:, :, head_cols(p, kv)],
                    send_sem=send_sem.at[kv, 0], recv_sem=recv_sem.at[kv, p],
                    device_id=(dp, p), device_id_type=MESH,
                ).wait_recv()
            own_store(kv, which).wait()

    def mate_copy(kv, t):
        return pltpu.make_async_remote_copy(
            src_ref=mate_out.at[kv, t], dst_ref=mate_in.at[kv, t],
            send_sem=mate_send.at[kv, t], recv_sem=mate_recv.at[kv, t],
            device_id=(mate, seq), device_id_type=MESH,
        )

    def chain_copy(kv, t, down):
        return pltpu.make_async_remote_copy(
            src_ref=chain_out.at[kv, t], dst_ref=(down_in if down else up_in).at[kv, t],
            send_sem=chain_send.at[kv, t], recv_sem=(down_recv if down else up_recv).at[kv, t],
            device_id=(below if down else above, seq), device_id_type=MESH,
        )

    def product(kv, which, store):
        @pl.loop(0, depth // tile)
        def _(i):
            cols = pl.ds(pl.multiple_of(which * depth + i * tile, tile), tile)
            rows = hid[:, :, :, cols].reshape(total, tile)
            part = jnp.dot(pre_t[kv], rows, preferred_element_type=f32)
            store(pl.ds(pl.multiple_of(i * tile, tile), tile), part)

    strip = 32

    def sweep(fn):
        @pl.loop(0, height // strip)
        def _(i):
            fn(pl.ds(pl.multiple_of(i * strip, strip), strip))

    def relay(kv, t, down, has_input):
        mate_copy(kv, t).wait_recv()

        def merge(extra):
            def fn(rows):
                v = acc[kv, t, rows, :]
                for e in (mate_in,) + extra:
                    v = v + e[kv, t, rows, :].astype(f32)
                chain_out[kv, t, rows, :] = v.astype(bf16)

            sweep(fn)

        if has_input:
            chain_copy(kv, t, down).wait_recv()
            merge((down_in if down else up_in,))
        else:
            merge(())
        chain_copy(kv, t, down).start()

    is_end = jnp.logical_or(chip == 0, chip == chips - 1)

    flip = lax.div(chips - 1 - chip, max(chips - 1, 1)) if chips > 1 else 0

    def turn(i):
        odd, k = lax.rem(i, 2), lax.div(i, 2)
        t = odd * (chips - 1 - k) + (1 - odd) * k
        return flip * (chips - 1 - t) + (1 - flip) * t

    def early(kv, t):
        @pl.when(jnp.logical_and(chip == chips - 1, t < chip))
        def _():
            relay(kv, t, True, False)

        @pl.when(jnp.logical_and(chip == 0, t > chip))
        def _():
            relay(kv, t, False, False)

    def products(kv):
        @pl.loop(0, chips)
        def _(i):
            t = turn(i)

            def to_mate(cols, part):
                mate_out[kv, t, :, cols] = part.astype(bf16)

            def to_acc(cols, part):
                acc[kv, t, :, cols] = part

            product(kv, t * CORES + 1 - core, to_mate)
            mate_copy(kv, t).start()
            product(kv, t * CORES + core, to_acc)

            @pl.when(i > 0)
            def _():
                early(kv, turn(i - 1))

        early(kv, turn(chips - 1))

    def chain(kv, cond):
        @pl.when(cond)
        def _():
            @pl.loop(0, chips - 1)
            def _(tau):
                k_down = tau - (chips - 1 - chip)
                k_up = tau - chip

                @pl.when(jnp.logical_and(k_down >= 0, k_down < chip))
                def _():
                    relay(kv, k_down, True, True)

                @pl.when(jnp.logical_and(k_up >= 0, k_up < chips - 1 - chip))
                def _():
                    relay(kv, chips - 1 - k_up, False, True)

    def prepare(kv):
        mate_copy(kv, chip).wait_recv()

        def fn(rows):
            acc[kv, chip, rows, :] += mate_in[kv, chip, rows, :].astype(f32)

        sweep(fn)

    def finish(kv):
        lanes = pl.ds(kv * HEAD_WIDTH, HEAD_WIDTH)

        def put(extra):
            @pl.loop(0, depth // HEAD_WIDTH)
            def _(j):
                at = pl.ds(pl.multiple_of(j * HEAD_WIDTH, HEAD_WIDTH), HEAD_WIDTH)
                v = acc[kv, chip, :, at]
                for e in extra:
                    v = v + e[kv, chip, :, at].astype(f32)
                key_grad[at, lanes] = v[:HEAD_WIDTH, :].T
                val_grad[at, lanes] = v[HEAD_WIDTH:, :].T

        if chips == 1:
            put(())
            return

        @pl.when(has_above)
        def _():
            chain_copy(kv, chip, True).wait_recv()

        @pl.when(has_below)
        def _():
            chain_copy(kv, chip, False).wait_recv()

        @pl.when(chip == 0)
        def _():
            put((down_in,))

        @pl.when(chip == chips - 1)
        def _():
            put((up_in,))

        @pl.when(jnp.logical_not(is_end))
        def _():
            put((down_in, up_in))

    for kv in range(kv_heads):
        project(kv)
        attend(kv)
        products(kv)
        give_back(kv)
    for kv in range(kv_heads):
        prepare(kv)
        chain(kv, jnp.logical_not(is_end))
    for kv in range(kv_heads):
        wait_back(kv)
        finish(kv)
    for copy in sends:
        copy.wait_send()
    for kind in range(2):
        for step in range(max(chips - 1, 1)):
            low, high = dp - CORES * step, dp + CORES * step
            go(jnp.logical_and(has_above, chip >= step),
               lambda: weight_copy(kind, low, above, up_send.at[step, kind]), True)
            go(jnp.logical_and(has_below, chip + step < chips),
               lambda: weight_copy(kind, high, below, down_send.at[step, kind]), True)
        for other in range(chips):
            piece = other * CORES + core
            weight_copy(kind, piece, mate, mate_w_send.at[piece, kind]).wait_send()
    for kv in range(kv_heads):
        for t in range(chips):
            mate_copy(kv, t).wait_send()
            go(chip != t, lambda: chain_copy(kv, t, True), True)


def local(n_seq, n_dp, hidden, queries, key_matrix, value_matrix, out_grad):
    _, stretches, tokens, embed = hidden.shape
    full = queries.shape[3]
    width = full // n_seq
    deep, kv_width = key_matrix.shape
    kv_heads = kv_width // HEAD_WIDTH
    group = width // kv_width
    wide = group * HEAD_WIDTH
    chips = n_dp // CORES
    rows, cols = grid_of(n_seq)
    hid_sends = 2 * (rows - 1 + cols - 1) + 2 * (rows - 1) * (cols - 1)
    total = stretches * n_seq * tokens
    bf16, f32 = jnp.bfloat16, jnp.float32
    dma = pltpu.SemaphoreType.DMA
    half = HEAD_WIDTH // 2
    inverse = np.exp(
        np.arange(half, dtype=np.float32) * np.float32(-2.0 * math.log(ROPE_BASE) / HEAD_WIDTH)
    ).astype(np.float32)
    phase = np.arange(total, dtype=np.float32)[:, None] * inverse[None, :]
    cos_half, sin_half = np.cos(phase), np.sin(phase)
    cos = np.concatenate([cos_half, cos_half], axis=1).astype(np.float32)
    sin = np.concatenate([-sin_half, sin_half], axis=1).astype(np.float32)
    heads = (kv_heads, stretches, n_seq, tokens, wide)
    single = (kv_heads * group, stretches, n_seq, tokens, HEAD_WIDTH)
    height = 2 * HEAD_WIDTH
    blocks = (kv_heads, chips, height, deep)
    weights = (n_dp, deep, kv_width)
    attn_out, query_grad, key_grad, val_grad = pl.pallas_call(
        functools.partial(kernel, n_seq, n_dp, kv_heads, group, math.gcd(deep, 256)),
        out_shape=[
            pltpu.VMEM((stretches, tokens, full), bf16),
            pltpu.VMEM((stretches, tokens, full), bf16),
            pltpu.VMEM((deep, kv_width), f32),
            pltpu.VMEM((deep, kv_width), f32),
        ],
        in_specs=[ANY] * 5 + [VMEM] * 4,
        out_specs=[VMEM] * 4,
        scratch_shapes=[
            pltpu.VMEM((stretches, n_seq, tokens, embed), bf16),
            pltpu.VMEM(single, bf16),
            pltpu.VMEM(single, bf16),
            pltpu.VMEM(weights, bf16),
            pltpu.VMEM(weights, bf16),
            pltpu.VMEM((total, 2 * HEAD_WIDTH), f32),
            pltpu.VMEM((total, kv_width), bf16),
            pltpu.VMEM((total, kv_width), bf16),
            pltpu.VMEM(heads, bf16),
            pltpu.VMEM(heads, bf16),
            pltpu.VMEM((kv_heads, height, total), bf16),
            pltpu.VMEM((HEAD_WIDTH, total), f32),
            pltpu.VMEM((HEAD_WIDTH, total), f32),
            pltpu.VMEM(blocks, f32),
            pltpu.VMEM(blocks, bf16),
            pltpu.VMEM(blocks, bf16),
            pltpu.VMEM(blocks, bf16),
            pltpu.VMEM(blocks, bf16),
            pltpu.VMEM(blocks, bf16),
            dma((3,)), dma((2, kv_heads * group)), dma((2, kv_heads)),
            dma((hid_sends,)), dma((n_seq, 2)),
            dma((kv_heads * group, n_seq)), dma((kv_heads * group, n_seq)),
            dma((kv_heads * group, n_seq)), dma((kv_heads * group, n_seq)),
            dma((chips, 2)), dma((chips, 2)), dma((n_dp, 2)), dma((n_dp, 2)),
            dma((kv_heads, n_seq)), dma((kv_heads, n_seq)),
            dma((kv_heads, n_seq)), dma((kv_heads, n_seq)),
            dma((kv_heads, chips)), dma((kv_heads, chips)), dma((kv_heads, chips)),
            dma((kv_heads, chips)), dma((kv_heads, chips)),
        ],
        compiler_params=pltpu.CompilerParams(
            collective_id=0, has_side_effects=True, vmem_limit_bytes=VMEM_LIMIT
        ),
        name="attention_step",
    )(hidden[0], queries[0], key_matrix, value_matrix, out_grad[0],
      cos, sin, cos.T.copy(), sin.T.copy())
    return attn_out[None], query_grad[None], key_grad, val_grad


def solution(mesh):
    n_dp, n_seq = mesh.shape["dp"], mesh.shape["seq"]
    tokens, weights = P("dp", None, "seq", None), P("dp", "seq")
    return jax.shard_map(
        functools.partial(local, n_seq, n_dp),
        mesh=mesh,
        in_specs=(tokens, tokens, weights, weights, tokens),
        out_specs=(tokens, tokens, weights, weights),
        check_vma=False,
    )
```

```python
import functools
import math

import jax
import jax.numpy as jnp
import numpy as np
from jax import lax
from jax.experimental import pallas as pl
from jax.experimental.pallas import tpu as pltpu
from jax.sharding import PartitionSpec as P

HEAD_WIDTH = 128
ROPE_BASE = 500000.0
CORES = 2
MESH = pl.DeviceIdType.MESH
ANY = pl.BlockSpec(memory_space=pl.ANY)
VMEM = pl.BlockSpec(memory_space=pltpu.VMEM)
VMEM_LIMIT = 56 << 20


def grid_of(count):
    rows = 2 if count % 2 == 0 else 1
    return rows, count // rows


def place(n_seq, n_dp):
    dp, seq = lax.axis_index("dp"), lax.axis_index("seq")
    chips = n_dp // CORES
    chip, core = lax.div(dp, CORES), lax.rem(dp, CORES)
    rows, cols = grid_of(n_seq)
    row, col = lax.div(seq, cols), lax.rem(seq, cols)
    row_peers = [row * cols + lax.rem(col + d, cols) for d in range(1, cols)]
    col_peers = [lax.rem(row + d, rows) * cols + col for d in range(1, rows)]
    far_peers = [
        lax.rem(row + e, rows) * cols + lax.rem(col + d, cols)
        for e in range(1, rows)
        for d in range(1, cols)
    ]
    return dp, seq, chips, chip, core, row_peers, col_peers, far_peers


def greet(dp, seq, chips, chip, core, peers):
    barrier = pltpu.get_barrier_semaphore()
    ids = [(dp, p) for p in peers]
    ids.append((chip * CORES + 1 - core, seq))
    if chips > 1:
        for d in (1, chips - 1):
            ids.append((lax.rem(chip + d, chips) * CORES + core, seq))
    for device in ids:
        pl.semaphore_signal(barrier, inc=1, device_id=device, device_id_type=MESH)
    pl.semaphore_wait(barrier, len(ids))


def kernel(
    n_seq, n_dp, kv_heads, group, tile,
    hidden, queries, key_matrix, value_matrix, out_grad, cos, sin, cos_t, sin_t,
    attn_out, qgrad_out, key_grad, val_grad,
    hid, qry, grd, key_all, val_all, raw_both, keys, vals, attn, qgrad, pre_t,
    key_acc, val_acc, acc, mate_out, mate_in, chain_out, down_in, up_in,
    load_sem, own_sem, store_sem, hid_send, hid_recv, qry_send, qry_recv, grd_send, grd_recv,
    up_send, down_send, mate_w_send, w_recv, a_send, a_recv, q_send, q_recv,
    mate_send, mate_recv, chain_send, down_recv, up_recv,
):
    f32, bf16 = jnp.float32, jnp.bfloat16
    dp, seq, chips, chip, core, row_peers, col_peers, far_peers = place(n_seq, n_dp)
    peers = row_peers + col_peers + far_peers
    above, below = dp + CORES, dp - CORES
    mate = chip * CORES + 1 - core
    has_above, has_below = chip < chips - 1, chip > 0
    wide = group * HEAD_WIDTH
    width = kv_heads * wide
    total = keys.shape[0]
    half = HEAD_WIDTH // 2
    block = total // 2

    def head_cols(target, kv):
        return pl.ds(pl.multiple_of(target * width + kv * wide, wide), wide)

    def one_head(target, h):
        start = pl.multiple_of(target * width + h * HEAD_WIDTH, HEAD_WIDTH)
        return pl.ds(start, HEAD_WIDTH)

    loads = [
        (hidden, hid.at[:, seq], load_sem.at[0]),
        (key_matrix, key_all.at[dp], load_sem.at[1]),
        (value_matrix, val_all.at[dp], load_sem.at[2]),
    ]

    def own_loads(h):
        return (
            (queries.at[:, :, one_head(seq, h)], qry.at[h, :, seq], own_sem.at[0, h]),
            (out_grad.at[:, :, one_head(seq, h)], grd.at[h, :, seq], own_sem.at[1, h]),
        )

    greet(dp, seq, chips, chip, core, peers)
    sends = []
    slots = iter(range(hid_send.shape[0]))

    def send_hidden(source, part, target, src):
        copy = pltpu.make_async_remote_copy(
            src_ref=src, dst_ref=hid.at[part, source],
            send_sem=hid_send.at[next(slots)], recv_sem=hid_recv.at[source, part],
            device_id=(dp, target), device_id_type=MESH,
        )
        copy.start()
        sends.append(copy)

    def wait_hidden(source, part):
        pltpu.make_async_remote_copy(
            src_ref=hid.at[part, source], dst_ref=hid.at[part, source],
            send_sem=hid_send.at[0], recv_sem=hid_recv.at[source, part],
            device_id=(dp, source), device_id_type=MESH,
        ).wait_recv()

    tables = (key_all, val_all)
    owns = (key_matrix, value_matrix)

    def weight_copy(kind, piece, target_dp, send_sem, own=False):
        return pltpu.make_async_remote_copy(
            src_ref=owns[kind] if own else tables[kind].at[piece],
            dst_ref=tables[kind].at[piece],
            send_sem=send_sem, recv_sem=w_recv.at[piece, kind],
            device_id=(target_dp, seq), device_id_type=MESH,
        )

    def go(cond, copy_of, wait=False):
        @pl.when(cond)
        def _():
            copy = copy_of()
            copy.wait_send() if wait else copy.start()

    for p in row_peers:
        send_hidden(seq, 0, p, hidden.at[0])
    for p in col_peers:
        send_hidden(seq, 1, p, hidden.at[1])
    for kind in range(2):
        go(has_above, lambda: weight_copy(kind, dp, above, up_send.at[0, kind], True))
        go(has_below, lambda: weight_copy(kind, dp, below, down_send.at[0, kind], True))
    for p in row_peers:
        send_hidden(seq, 1, p, hidden.at[1])
    for p in col_peers:
        send_hidden(seq, 0, p, hidden.at[0])
    for kind in range(2):
        weight_copy(kind, dp, mate, mate_w_send.at[dp, kind], True).start()
    for copy in loads + [c for h in range(kv_heads * group) for c in own_loads(h)]:
        pltpu.make_async_copy(*copy).start()

    def relay_weight(step, kind):
        low, high = dp - CORES * step, dp + CORES * step

        @pl.when(chip >= step)
        def _():
            weight_copy(kind, low, below, up_send.at[step, kind]).wait_recv()
            go(has_above, lambda: weight_copy(kind, low, above, up_send.at[step, kind]))
            weight_copy(kind, low, mate, mate_w_send.at[low, kind]).start()

        @pl.when(chip + step < chips)
        def _():
            weight_copy(kind, high, above, down_send.at[step, kind]).wait_recv()
            go(has_below, lambda: weight_copy(kind, high, below, down_send.at[step, kind]))
            weight_copy(kind, high, mate, mate_w_send.at[high, kind]).start()

    def relay_hidden():
        for p in row_peers:
            wait_hidden(p, 0)
            for q in col_peers:
                send_hidden(p, 0, q, hid.at[0, p])
        for p in col_peers:
            wait_hidden(p, 1)
            for q in row_peers:
                send_hidden(p, 1, q, hid.at[1, p])

    def exchange(h, src, dst, send_sem, recv_sem):
        for i, p in enumerate(peers):
            copy = pltpu.make_async_remote_copy(
                src_ref=src.at[:, :, one_head(p, h)], dst_ref=dst.at[h, :, seq],
                send_sem=send_sem.at[h, i], recv_sem=recv_sem.at[h, seq],
                device_id=(dp, p), device_id_type=MESH,
            )
            copy.start()
            sends.append(copy)

    def wait_exchange(h, dst, send_sem, recv_sem):
        for p in peers:
            pltpu.make_async_remote_copy(
                src_ref=dst.at[h, :, p], dst_ref=dst.at[h, :, p],
                send_sem=send_sem.at[h, 0], recv_sem=recv_sem.at[h, p],
                device_id=(dp, p), device_id_type=MESH,
            ).wait_recv()

    if chips > 1:
        relay_weight(1, 0)
    relay_hidden()
    for h in range(kv_heads * group):
        exchange(h, queries, qry, qry_send, qry_recv)
        exchange(h, out_grad, grd, grd_send, grd_recv)
    if chips > 1:
        relay_weight(1, 1)
    for step in range(2, chips):
        for kind in range(2):
            relay_weight(step, kind)
    for p in row_peers:
        wait_hidden(p, 1)
    for p in col_peers:
        wait_hidden(p, 0)
    for p in far_peers:
        wait_hidden(p, 0)
        wait_hidden(p, 1)
    for other in range(chips):
        for kind in range(2):
            piece = other * CORES + 1 - core
            weight_copy(kind, piece, mate, mate_w_send.at[piece, kind]).wait_recv()
    for copy in loads:
        pltpu.make_async_copy(*copy).wait()

    deep = key_all.shape[1]

    def project(kv):
        lanes = pl.ds(kv * HEAD_WIDTH, HEAD_WIDTH)
        raw_both[...] = jnp.zeros_like(raw_both)

        @pl.loop(0, n_dp)
        def _(d):
            cols = pl.ds(pl.multiple_of(d * deep, deep), deep)
            rows = hid[:, :, :, cols].reshape(total, deep)
            both = jnp.concatenate([key_all[d, :, lanes], val_all[d, :, lanes]], axis=1)
            raw_both[...] += jnp.dot(rows, both, preferred_element_type=f32)

        raw = raw_both[:, :HEAD_WIDTH]
        swapped = jnp.concatenate([raw[:, half:], raw[:, :half]], axis=1)
        keys[:, lanes] = (raw * cos[...] + swapped * sin[...]).astype(bf16)
        vals[:, lanes] = raw_both[:, HEAD_WIDTH:].astype(bf16)

    scale = 1.0 / math.sqrt(HEAD_WIDTH)
    nt = (((1,), (1,)), ((), ()))
    tn = (((0,), (0,)), ((), ()))

    def attend(kv):
        lanes = pl.ds(kv * HEAD_WIDTH, HEAD_WIDTH)
        key_acc[...] = jnp.zeros_like(key_acc)
        val_acc[...] = jnp.zeros_like(val_acc)

        @pl.loop(0, group)
        def _(m):
            head = pl.ds(pl.multiple_of(m * HEAD_WIDTH, HEAD_WIDTH), HEAD_WIDTH)
            h = kv * group + m
            wait_exchange(h, qry, qry_send, qry_recv)
            wait_exchange(h, grd, grd_send, grd_recv)
            for copy in own_loads(h):
                pltpu.make_async_copy(*copy).wait()
            for b in range(2):
                span = (b + 1) * block
                q = qry[h, b].reshape(block, HEAD_WIDTH)
                g = grd[h, b].reshape(block, HEAD_WIDTH)
                k, v = keys[:span, lanes], vals[:span, lanes]
                s = lax.dot_general(q, k, nt, preferred_element_type=f32) * scale
                at = b * block + lax.broadcasted_iota(jnp.int32, s.shape, 0)
                col = lax.broadcasted_iota(jnp.int32, s.shape, 1)
                s = jnp.where(col <= at, s, -jnp.inf)
                e = jnp.exp(s - jnp.max(s, axis=1, keepdims=True))
                p = e * (1.0 / jnp.sum(e, axis=1, keepdims=True))
                p_half = p.astype(bf16)
                o = jnp.dot(p_half, v, preferred_element_type=f32).astype(bf16)
                attn[kv, b, :, :, head] = o.reshape(n_seq, block // n_seq, HEAD_WIDTH)
                dot = jnp.sum(g.astype(f32) * o.astype(f32), axis=1, keepdims=True)
                gp = lax.dot_general(g, v, nt, preferred_element_type=f32)
                ds = (p * (gp - dot) * scale).astype(bf16)
                dq = jnp.dot(ds, k, preferred_element_type=f32).astype(bf16)
                qgrad[kv, b, :, :, head] = dq.reshape(n_seq, block // n_seq, HEAD_WIDTH)
                key_acc[:, :span] += lax.dot_general(q, ds, tn, preferred_element_type=f32)
                val_acc[:, :span] += lax.dot_general(g, p_half, tn, preferred_element_type=f32)

        grown = key_acc[...]
        swapped = jnp.concatenate([grown[half:, :], grown[:half, :]], axis=0)
        pre_t[kv, :HEAD_WIDTH, :] = (grown * cos_t[...] - swapped * sin_t[...]).astype(bf16)
        pre_t[kv, HEAD_WIDTH:, :] = val_acc[...].astype(bf16)

    height, depth = acc.shape[2], acc.shape[3]
    results = ((attn, attn_out, a_send, a_recv), (qgrad, qgrad_out, q_send, q_recv))

    def own_store(kv, which):
        src, dst, _, _ = results[which]
        return pltpu.make_async_copy(
            src.at[kv, :, seq], dst.at[:, :, head_cols(seq, kv)], store_sem.at[which, kv]
        )

    def give_back(kv):
        for which, (src, dst, send_sem, recv_sem) in enumerate(results):
            for i, p in enumerate(peers):
                copy = pltpu.make_async_remote_copy(
                    src_ref=src.at[kv, :, p], dst_ref=dst.at[:, :, head_cols(seq, kv)],
                    send_sem=send_sem.at[kv, i], recv_sem=recv_sem.at[kv, seq],
                    device_id=(dp, p), device_id_type=MESH,
                )
                copy.start()
                sends.append(copy)
            own_store(kv, which).start()

    def wait_back(kv):
        for which, (src, dst, send_sem, recv_sem) in enumerate(results):
            for p in peers:
                pltpu.make_async_remote_copy(
                    src_ref=src.at[kv, :, p], dst_ref=dst.at[:, :, head_cols(p, kv)],
                    send_sem=send_sem.at[kv, 0], recv_sem=recv_sem.at[kv, p],
                    device_id=(dp, p), device_id_type=MESH,
                ).wait_recv()
            own_store(kv, which).wait()

    def mate_copy(kv, t):
        return pltpu.make_async_remote_copy(
            src_ref=mate_out.at[kv, t], dst_ref=mate_in.at[kv, t],
            send_sem=mate_send.at[kv, t], recv_sem=mate_recv.at[kv, t],
            device_id=(mate, seq), device_id_type=MESH,
        )

    def chain_copy(kv, t, down):
        return pltpu.make_async_remote_copy(
            src_ref=chain_out.at[kv, t], dst_ref=(down_in if down else up_in).at[kv, t],
            send_sem=chain_send.at[kv, t], recv_sem=(down_recv if down else up_recv).at[kv, t],
            device_id=(below if down else above, seq), device_id_type=MESH,
        )

    def product(kv, which, store):
        @pl.loop(0, depth // tile)
        def _(i):
            cols = pl.ds(pl.multiple_of(which * depth + i * tile, tile), tile)
            rows = hid[:, :, :, cols].reshape(total, tile)
            part = jnp.dot(pre_t[kv], rows, preferred_element_type=f32)
            store(pl.ds(pl.multiple_of(i * tile, tile), tile), part)

    strip = 32

    def sweep(fn):
        @pl.loop(0, height // strip)
        def _(i):
            fn(pl.ds(pl.multiple_of(i * strip, strip), strip))

    def relay(kv, t, down, has_input):
        mate_copy(kv, t).wait_recv()

        def merge(extra):
            def fn(rows):
                v = acc[kv, t, rows, :]
                for e in (mate_in,) + extra:
                    v = v + e[kv, t, rows, :].astype(f32)
                chain_out[kv, t, rows, :] = v.astype(bf16)

            sweep(fn)

        if has_input:
            chain_copy(kv, t, down).wait_recv()
            merge((down_in if down else up_in,))
        else:
            merge(())
        chain_copy(kv, t, down).start()

    is_end = jnp.logical_or(chip == 0, chip == chips - 1)

    flip = lax.div(chips - 1 - chip, max(chips - 1, 1)) if chips > 1 else 0

    def turn(i):
        odd, k = lax.rem(i, 2), lax.div(i, 2)
        t = odd * (chips - 1 - k) + (1 - odd) * k
        return flip * (chips - 1 - t) + (1 - flip) * t

    def early(kv, t):
        @pl.when(jnp.logical_and(chip == chips - 1, t < chip))
        def _():
            relay(kv, t, True, False)

        @pl.when(jnp.logical_and(chip == 0, t > chip))
        def _():
            relay(kv, t, False, False)

    def products(kv):
        @pl.loop(0, chips)
        def _(i):
            t = turn(i)

            def to_mate(cols, part):
                mate_out[kv, t, :, cols] = part.astype(bf16)

            def to_acc(cols, part):
                acc[kv, t, :, cols] = part

            product(kv, t * CORES + 1 - core, to_mate)
            mate_copy(kv, t).start()
            product(kv, t * CORES + core, to_acc)

            @pl.when(i > 0)
            def _():
                early(kv, turn(i - 1))

        early(kv, turn(chips - 1))

    def chain(kv, cond):
        @pl.when(cond)
        def _():
            @pl.loop(0, chips - 1)
            def _(tau):
                k_down = tau - (chips - 1 - chip)
                k_up = tau - chip

                @pl.when(jnp.logical_and(k_down >= 0, k_down < chip))
                def _():
                    relay(kv, k_down, True, True)

                @pl.when(jnp.logical_and(k_up >= 0, k_up < chips - 1 - chip))
                def _():
                    relay(kv, chips - 1 - k_up, False, True)

    def prepare(kv):
        mate_copy(kv, chip).wait_recv()

        def fn(rows):
            acc[kv, chip, rows, :] += mate_in[kv, chip, rows, :].astype(f32)

        sweep(fn)

    def finish(kv):
        lanes = pl.ds(kv * HEAD_WIDTH, HEAD_WIDTH)

        def put(extra):
            @pl.loop(0, depth // HEAD_WIDTH)
            def _(j):
                at = pl.ds(pl.multiple_of(j * HEAD_WIDTH, HEAD_WIDTH), HEAD_WIDTH)
                v = acc[kv, chip, :, at]
                for e in extra:
                    v = v + e[kv, chip, :, at].astype(f32)
                key_grad[at, lanes] = v[:HEAD_WIDTH, :].T
                val_grad[at, lanes] = v[HEAD_WIDTH:, :].T

        if chips == 1:
            put(())
            return

        @pl.when(has_above)
        def _():
            chain_copy(kv, chip, True).wait_recv()

        @pl.when(has_below)
        def _():
            chain_copy(kv, chip, False).wait_recv()

        @pl.when(chip == 0)
        def _():
            put((down_in,))

        @pl.when(chip == chips - 1)
        def _():
            put((up_in,))

        @pl.when(jnp.logical_not(is_end))
        def _():
            put((down_in, up_in))

    for kv in range(kv_heads):
        project(kv)
        attend(kv)
        products(kv)
        give_back(kv)
    for kv in range(kv_heads):
        prepare(kv)
        chain(kv, jnp.logical_not(is_end))
    for kv in range(kv_heads):
        wait_back(kv)
        finish(kv)
    for copy in sends:
        copy.wait_send()
    for kind in range(2):
        for step in range(max(chips - 1, 1)):
            low, high = dp - CORES * step, dp + CORES * step
            go(jnp.logical_and(has_above, chip >= step),
               lambda: weight_copy(kind, low, above, up_send.at[step, kind]), True)
            go(jnp.logical_and(has_below, chip + step < chips),
               lambda: weight_copy(kind, high, below, down_send.at[step, kind]), True)
        for other in range(chips):
            piece = other * CORES + core
            weight_copy(kind, piece, mate, mate_w_send.at[piece, kind]).wait_send()
    for kv in range(kv_heads):
        for t in range(chips):
            mate_copy(kv, t).wait_send()
            go(chip != t, lambda: chain_copy(kv, t, True), True)


def put_kernel(*refs):
    count = len(refs) // 2
    sem = refs[-1]
    copies = [
        pltpu.make_async_copy(refs[i], refs[count + i], sem.at[i]) for i in range(count)
    ]
    for copy in copies:
        copy.start()
    for copy in copies:
        copy.wait()


def put_all(*arrays):
    return pl.pallas_call(
        put_kernel,
        out_shape=[jax.ShapeDtypeStruct(x.shape, x.dtype) for x in arrays],
        in_specs=[pl.BlockSpec(memory_space=pltpu.VMEM)] * len(arrays),
        out_specs=[ANY] * len(arrays),
        scratch_shapes=[pltpu.SemaphoreType.DMA((len(arrays),))],
        compiler_params=pltpu.CompilerParams(vmem_limit_bytes=1 << 20),
        name="put_all",
    )(*arrays)


def local(n_seq, n_dp, hidden, queries, key_matrix, value_matrix, out_grad):
    _, stretches, tokens, embed = hidden.shape
    full = queries.shape[3]
    width = full // n_seq
    deep, kv_width = key_matrix.shape
    kv_heads = kv_width // HEAD_WIDTH
    group = width // kv_width
    wide = group * HEAD_WIDTH
    chips = n_dp // CORES
    rows, cols = grid_of(n_seq)
    hid_sends = 2 * (rows - 1 + cols - 1) + 2 * (rows - 1) * (cols - 1)
    total = stretches * n_seq * tokens
    bf16, f32 = jnp.bfloat16, jnp.float32
    dma = pltpu.SemaphoreType.DMA
    half = HEAD_WIDTH // 2
    inverse = np.exp(
        np.arange(half, dtype=np.float32) * np.float32(-2.0 * math.log(ROPE_BASE) / HEAD_WIDTH)
    ).astype(np.float32)
    phase = np.arange(total, dtype=np.float32)[:, None] * inverse[None, :]
    cos_half, sin_half = np.cos(phase), np.sin(phase)
    cos = np.concatenate([cos_half, cos_half], axis=1).astype(np.float32)
    sin = np.concatenate([-sin_half, sin_half], axis=1).astype(np.float32)
    heads = (kv_heads, stretches, n_seq, tokens, wide)
    single = (kv_heads * group, stretches, n_seq, tokens, HEAD_WIDTH)
    height = 2 * HEAD_WIDTH
    blocks = (kv_heads, chips, height, deep)
    weights = (n_dp, deep, kv_width)
    attn_out, query_grad, key_grad, val_grad = pl.pallas_call(
        functools.partial(kernel, n_seq, n_dp, kv_heads, group, math.gcd(deep, 256)),
        out_shape=[
            pltpu.VMEM((stretches, tokens, full), bf16),
            pltpu.VMEM((stretches, tokens, full), bf16),
            pltpu.VMEM((deep, kv_width), f32),
            pltpu.VMEM((deep, kv_width), f32),
        ],
        in_specs=[ANY] * 5 + [VMEM] * 4,
        out_specs=[VMEM] * 4,
        scratch_shapes=[
            pltpu.VMEM((stretches, n_seq, tokens, embed), bf16),
            pltpu.VMEM(single, bf16),
            pltpu.VMEM(single, bf16),
            pltpu.VMEM(weights, bf16),
            pltpu.VMEM(weights, bf16),
            pltpu.VMEM((total, 2 * HEAD_WIDTH), f32),
            pltpu.VMEM((total, kv_width), bf16),
            pltpu.VMEM((total, kv_width), bf16),
            pltpu.VMEM(heads, bf16),
            pltpu.VMEM(heads, bf16),
            pltpu.VMEM((kv_heads, height, total), bf16),
            pltpu.VMEM((HEAD_WIDTH, total), f32),
            pltpu.VMEM((HEAD_WIDTH, total), f32),
            pltpu.VMEM(blocks, f32),
            pltpu.VMEM(blocks, bf16),
            pltpu.VMEM(blocks, bf16),
            pltpu.VMEM(blocks, bf16),
            pltpu.VMEM(blocks, bf16),
            pltpu.VMEM(blocks, bf16),
            dma((3,)), dma((2, kv_heads * group)), dma((2, kv_heads)),
            dma((hid_sends,)), dma((n_seq, 2)),
            dma((kv_heads * group, n_seq)), dma((kv_heads * group, n_seq)),
            dma((kv_heads * group, n_seq)), dma((kv_heads * group, n_seq)),
            dma((chips, 2)), dma((chips, 2)), dma((n_dp, 2)), dma((n_dp, 2)),
            dma((kv_heads, n_seq)), dma((kv_heads, n_seq)),
            dma((kv_heads, n_seq)), dma((kv_heads, n_seq)),
            dma((kv_heads, chips)), dma((kv_heads, chips)), dma((kv_heads, chips)),
            dma((kv_heads, chips)), dma((kv_heads, chips)),
        ],
        compiler_params=pltpu.CompilerParams(
            collective_id=0, has_side_effects=True, vmem_limit_bytes=VMEM_LIMIT
        ),
        name="attention_step",
    )(hidden[0], queries[0], key_matrix, value_matrix, out_grad[0],
      cos, sin, cos.T.copy(), sin.T.copy())
    attn_out, query_grad, key_grad, val_grad = put_all(
        attn_out, query_grad, key_grad, val_grad
    )
    return attn_out[None], query_grad[None], key_grad, val_grad


def solution(mesh):
    n_dp, n_seq = mesh.shape["dp"], mesh.shape["seq"]
    tokens, weights = P("dp", None, "seq", None), P("dp", "seq")
    return jax.shard_map(
        functools.partial(local, n_seq, n_dp),
        mesh=mesh,
        in_specs=(tokens, tokens, weights, weights, tokens),
        out_specs=(tokens, tokens, weights, weights),
        check_vma=False,
    )
```
